256 devices in a mesh: wide: 32 (over z, y), slab: 8 (over x, core).
Axes of the slice: x: 4, y: 4, z: 8, core: 2. Of those that a mesh axis runs over, the one named last changes fastest.
Arguments:
- thermal_state: float32 [32, 128, 32, 1024], P('wide', 'slab'), may hold values from -5 to 5
- thermal_spreading_rate: bfloat16 [32, 128, 32, 1024], P('wide', 'slab'), may hold values from 0.5 to 1.5
- flow_speed_vector: bfloat16 [3, 32, 128, 32, 1024], P(None, 'wide', 'slab'), may hold values from -0.796875 to 0.796875
- interface_guess: float32 [32, 2048], P('wide', 'slab'), may hold values from -4 to 4
- partner_facing_rows: int32 [32, 2048], P('wide', 'slab'), may hold values from 0 to 2047, each once within a row
- mismatch_change_matrix: float32 [32, 2048, 128], P('wide', 'slab'), may hold values from -5 to 5
- output_change_matrix: float32 [32, 2048, 128], P('wide', 'slab'), may hold values from -1.8 to 1.8
Outputs:
- temperature_out: float32 [32, 128, 32, 1024], P('wide', 'slab')
- updated_interface_guess: float32 [32, 2048], P('wide', 'slab')
- unitary_basis_factor: float32 [32, 2048, 128], P('wide', 'slab')
The draws below stay inside these ranges and needn't reach their ends.
Inputs may be any that keep to these rules, and one draw needn't show every extreme that they name: `partner_facing_rows`: each partition's rows of matching are a permutation of its partner's interface rows.
All inputs are finite; a program needn't handle non-finite values.
Results may differ from the reference program's by a relative error of at most 0.0003.
Values may be sent and summed in bfloat16 or wider, within the bound.
No kernel may reach another device: no remote copies, remote signals or barrier semaphores. Data moves between devices by JAX's collectives and lax.ppermute only.
A program may use at most 64 MiB of HBM per device.

```python
import jax
import jax.numpy as jnp
from jax import lax

GRID_SPAN_TWO = 32
GRID_SPAN_DEPTH = 1024
INTERFACE_STRIP = 64
COLS = 128
SWEEPS = 4
GRID_SPAN_ONE = 128
IFACE = 2048
N_WIDE = 32


def draw_mismatch_change_matrix(key, part):
    first_key, second_key, third_key = jax.random.split(key, 3)
    array_dimensions = (N_WIDE, IFACE, COLS)
    normal_part = jnp.clip(jax.random.normal(first_key, array_dimensions, jnp.float32), -5.0, 5.0)
    row_scales = 10.0 ** jax.random.uniform(second_key, (N_WIDE, IFACE, 1), jnp.float32)
    column_scales = 10.0 ** jax.random.uniform(third_key, (1, 1, COLS), jnp.float32)
    position = (jnp.arange(N_WIDE, dtype=jnp.float32)[:, None] * IFACE + jnp.arange(IFACE, dtype=jnp.float32)[None, :]) / (N_WIDE * IFACE)
    rising = 1.0 + 2.0 * position[:, :, None]
    return 0.0005 * normal_part * row_scales * column_scales * rising


def level_of(rng, shape, cuts, least, largest):
    level, own = 1.0, jax.random.fold_in(rng, 6)
    for dim, blocks in cuts:
        heights = jnp.exp(jax.random.uniform(jax.random.fold_in(own, dim), (blocks,), jnp.float32, least / len(cuts), largest / len(cuts)))
        level = level * jnp.repeat(heights, shape[dim] // blocks).reshape([-1 if axis == dim else 1 for axis in range(len(shape))])
    return level


def scatter_about(key, shape, scale, most, shards=(), held_as=jnp.bfloat16):
    gain = level_of(key, shape, shards, -0.22, 0.18) if shards else 1.0
    drawn = jax.random.normal(key, shape, jnp.float32) * scale * gain
    return jnp.minimum(jnp.maximum(drawn, -most), most).astype(held_as)


def setup_inputs(seed: int = 0) -> dict:
    splits = jax.random.split(jax.random.key(seed), 8)
    return {
        "thermal_state": scatter_about(splits[0], (N_WIDE, GRID_SPAN_ONE, GRID_SPAN_TWO, GRID_SPAN_DEPTH), 1.0, 5.0, ((0, 32), (1, 8)), jnp.float32),
        "thermal_spreading_rate": jnp.clip(0.5 + 1.0 * jax.random.uniform(splits[1], (N_WIDE, GRID_SPAN_ONE, GRID_SPAN_TWO, GRID_SPAN_DEPTH), jnp.float32) ** level_of(splits[1], (N_WIDE, GRID_SPAN_ONE, GRID_SPAN_TWO, GRID_SPAN_DEPTH), ((0, 32), (1, 8)), -0.2, 0.2), 0.5, 1.5).astype(jnp.bfloat16),
        "flow_speed_vector": jnp.clip(jax.random.uniform(splits[2], (3, N_WIDE, GRID_SPAN_ONE, GRID_SPAN_TWO, GRID_SPAN_DEPTH), jnp.float32, -0.796875, 0.796875) * level_of(splits[2], (3, N_WIDE, GRID_SPAN_ONE, GRID_SPAN_TWO, GRID_SPAN_DEPTH), ((1, 32), (2, 8)), -0.4, 0.0), -0.796875, 0.796875).astype(jnp.bfloat16),
        "interface_guess": scatter_about(splits[3], (N_WIDE, IFACE), 1.0, 4.0, ((0, 32), (1, 8)), jnp.float32),
        "partner_facing_rows": jax.vmap(lambda own: jax.random.permutation(own, IFACE))(jax.random.split(splits[4], N_WIDE)).reshape((N_WIDE, IFACE)).astype(jnp.int32),
        "mismatch_change_matrix": draw_mismatch_change_matrix(jax.random.fold_in(splits[7], 71), 0),
        "output_change_matrix": scatter_about(splits[6], (N_WIDE, IFACE, COLS), 0.3, 1.8, ((0, 32), (1, 8)), jnp.float32),
    }


STEP_SIZE = 0.11

def surround_wrapper(block_rows, mirror_layer):
    bottom = jnp.zeros((block_rows.shape[0], 1, block_rows.shape[2]), block_rows.dtype)
    stacked = jnp.concatenate([bottom, block_rows, mirror_layer[:, None, :]], axis=1)
    return jnp.pad(stacked, ((0, 0), (0, 0), (1, 1)))

def march_forward(bordered_array, diffuse_subdomain, subdomain_flow_speed):
    centre = bordered_array[1:-1, 1:-1, 1:-1]
    plus_first = bordered_array[2:, 1:-1, 1:-1]
    minus_first = bordered_array[:-2, 1:-1, 1:-1]
    plus_second = bordered_array[1:-1, 2:, 1:-1]
    minus_second = bordered_array[1:-1, :-2, 1:-1]
    plus_third = bordered_array[1:-1, 1:-1, 2:]
    minus_third = bordered_array[1:-1, 1:-1, :-2]
    spread = plus_first + minus_first + plus_second + minus_second + plus_third + minus_third - 6.0 * centre
    carried = 0.5 * (subdomain_flow_speed[0].astype(jnp.float32) * (plus_first - minus_first) + subdomain_flow_speed[1].astype(jnp.float32) * (plus_second - minus_second) + subdomain_flow_speed[2].astype(jnp.float32) * (plus_third - minus_third))
    return centre + STEP_SIZE * (diffuse_subdomain.astype(jnp.float32) * spread - carried)

def reference(thermal_state, thermal_spreading_rate, flow_speed_vector, interface_guess, partner_facing_rows, mismatch_change_matrix, output_change_matrix):
    ghost_all = jnp.repeat(interface_guess.reshape(N_WIDE, GRID_SPAN_ONE, GRID_SPAN_DEPTH // INTERFACE_STRIP), INTERFACE_STRIP, axis=2)

    def evolve(voxel_position):
        subdomain_thermal_state = thermal_state[voxel_position]
        diffuse_subdomain = thermal_spreading_rate[voxel_position]
        subdomain_flow_speed = flow_speed_vector[:, voxel_position]
        mirror_layer = jnp.pad(ghost_all[voxel_position], ((1, 1), (0, 0)))
        for sweep in range(SWEEPS):
            bordered_array = surround_wrapper(jnp.pad(subdomain_thermal_state, ((1, 1), (0, 0), (0, 0))), mirror_layer)
            subdomain_thermal_state = march_forward(bordered_array, diffuse_subdomain, subdomain_flow_speed)
        return subdomain_thermal_state
    final = lax.map(evolve, jnp.arange(N_WIDE))
    face_means = lax.optimization_barrier(jnp.mean(final[:, :, GRID_SPAN_TWO - 1, :].reshape(N_WIDE, GRID_SPAN_ONE, GRID_SPAN_DEPTH // INTERFACE_STRIP, INTERFACE_STRIP), axis=3))
    face_means = face_means.reshape(N_WIDE, IFACE)
    partner = jnp.roll(face_means, N_WIDE // 2, axis=0)
    tilde = jnp.take_along_axis(partner, partner_facing_rows, axis=1)
    resid = tilde - interface_guess
    flat = mismatch_change_matrix.reshape(N_WIDE * IFACE, COLS)
    gram_matrix = lax.dot_general(flat.astype(jnp.float32), flat.astype(jnp.float32), (((0,), (0,)), ((), ())), precision=lax.Precision.HIGHEST, preferred_element_type=jnp.float32)
    projection = jnp.dot(resid.reshape(N_WIDE * IFACE).astype(jnp.float32), flat.astype(jnp.float32), precision=lax.Precision.HIGHEST, preferred_element_type=jnp.float32)
    lower_factor = jnp.linalg.cholesky(gram_matrix)
    half_solve = lax.linalg.triangular_solve(lower_factor, projection[:, None], left_side=True, lower=True)
    coefficients = -lax.linalg.triangular_solve(lower_factor, half_solve, left_side=True, lower=True, transpose_a=True)[:, 0]
    update = jnp.dot(output_change_matrix.reshape(N_WIDE * IFACE, COLS).astype(jnp.float32), coefficients.astype(jnp.float32), precision=lax.Precision.HIGHEST, preferred_element_type=jnp.float32)
    updated_interface_guess = tilde + update.reshape(N_WIDE, IFACE)
    scaled = lax.linalg.triangular_solve(lower_factor, flat, left_side=False, lower=True, transpose_a=True)
    unitary_basis_factor = (jnp.sqrt(jnp.float32(N_WIDE * IFACE)) * scaled).reshape(N_WIDE, IFACE, COLS)
    return (final, updated_interface_guess, unitary_basis_factor)
```

```python
import math

import jax
import jax.numpy as jnp
from jax import lax
from jax.sharding import PartitionSpec as P

INTERFACE_STRIP = 64
SWEEPS = 4


STEP_SIZE = 0.11


def padded(cells, sides, width):
    for axis, dim in sides:
        count = lax.axis_size(axis)
        ends = count - 1
        head = lax.slice_in_dim(cells, 0, width, axis=dim)
        tail = lax.slice_in_dim(cells, cells.shape[dim] - width, cells.shape[dim], axis=dim)
        cells = jnp.concatenate(
            [
                lax.ppermute(tail, axis, [(i, (i + 1) % count) for i in range(ends)]),
                cells,
                lax.ppermute(head, axis, [((i + 1) % count, i) for i in range(ends)]),
            ],
            axis=dim,
        )
    return cells


def partner(value, axis, stride):
    mask = 2**stride
    pairs = [(source, source ^ mask) for source in range(lax.axis_size(axis))]
    return lax.ppermute(value, axis, pairs)


def gather_sum(value, axes):
    count = lax.axis_size(axes)
    copies = jnp.broadcast_to(value[None], (count, *value.shape))
    return jnp.sum(lax.all_to_all(copies, axes, 0, 0, tiled=True), axis=0)


def sum_everywhere(square):
    rows = square.shape[0] // lax.axis_size("slab")
    blocks = square.reshape(-1, rows, square.shape[1])
    mine = jnp.sum(lax.all_to_all(blocks, "slab", 0, 0, tiled=True), axis=0)
    mine = gather_sum(mine, "wide")
    copies = jnp.broadcast_to(mine[None], blocks.shape)
    return lax.all_to_all(copies, "slab", 0, 0, tiled=True).reshape(square.shape)


def surround_wrapper(block_rows, mirror_layer):
    bottom = jnp.zeros((block_rows.shape[0], 1, block_rows.shape[2]), block_rows.dtype)
    stacked = jnp.concatenate([bottom, block_rows, mirror_layer[:, None, :]], axis=1)
    return jnp.pad(stacked, ((0, 0), (0, 0), (1, 1)))


def march_forward(bordered_array, diffuse_subdomain, subdomain_flow_speed):
    centre = bordered_array[1:-1, 1:-1, 1:-1]
    plus_first = bordered_array[2:, 1:-1, 1:-1]
    minus_first = bordered_array[:-2, 1:-1, 1:-1]
    plus_second = bordered_array[1:-1, 2:, 1:-1]
    minus_second = bordered_array[1:-1, :-2, 1:-1]
    plus_third = bordered_array[1:-1, 1:-1, 2:]
    minus_third = bordered_array[1:-1, 1:-1, :-2]
    spread = (
        plus_first
        + minus_first
        + plus_second
        + minus_second
        + plus_third
        + minus_third
        - 6.0 * centre
    )
    carried = 0.5 * (
        subdomain_flow_speed[0].astype(jnp.float32) * (plus_first - minus_first)
        + subdomain_flow_speed[1].astype(jnp.float32) * (plus_second - minus_second)
        + subdomain_flow_speed[2].astype(jnp.float32) * (plus_third - minus_third)
    )
    return centre + STEP_SIZE * (diffuse_subdomain.astype(jnp.float32) * spread - carried)


def shards(
    thermal_state,
    thermal_spreading_rate,
    flow_speed_vector,
    interface_guess,
    partner_facing_rows,
    mismatch_change_matrix,
    output_change_matrix,
):
    subdomain_thermal_state = thermal_state[0]
    diffuse_subdomain = thermal_spreading_rate[0]
    subdomain_flow_speed = flow_speed_vector[:, 0]
    layer_stack = subdomain_thermal_state.shape[0]
    vertical_extent = subdomain_thermal_state.shape[1]
    rows_dev = interface_guess.shape[1]
    mirror_layer = jnp.repeat(interface_guess[0].reshape(layer_stack, -1), INTERFACE_STRIP, axis=1)
    panel = mismatch_change_matrix[0]
    gram_local = lax.dot_general(
        panel,
        panel,
        (((0,), (0,)), ((), ())),
        precision=lax.Precision.HIGHEST,
        preferred_element_type=jnp.float32,
    )
    ghost_padded = jnp.pad(mirror_layer, ((1, 1), (0, 0)))
    for sweep in range(SWEEPS):
        widened_array = padded(subdomain_thermal_state, (("slab", 0),), 1)
        subdomain_thermal_state = march_forward(
            surround_wrapper(widened_array, ghost_padded), diffuse_subdomain, subdomain_flow_speed
        )
    face_means = jnp.mean(
        subdomain_thermal_state[:, vertical_extent - 1, :].reshape(
            layer_stack, -1, INTERFACE_STRIP
        ),
        axis=2,
    )
    face_means = face_means.reshape(1, rows_dev)
    top_bit = lax.axis_size("wide").bit_length() - 2
    partner_own = partner(face_means, "wide", top_bit)
    partner_all = lax.all_gather(partner_own, "slab", axis=1, tiled=True)
    tilde = jnp.take(partner_all[0], partner_facing_rows[0], axis=0)
    resid = tilde - interface_guess[0]
    proj_local = jnp.dot(
        resid, panel, precision=lax.Precision.HIGHEST, preferred_element_type=jnp.float32
    )
    gram_matrix = sum_everywhere(gram_local)
    projection = gather_sum(proj_local, ("wide", "slab"))
    lower_factor = jnp.linalg.cholesky(gram_matrix)
    half_solve = lax.linalg.triangular_solve(
        lower_factor, projection[:, None], left_side=True, lower=True
    )
    coefficients = -lax.linalg.triangular_solve(
        lower_factor, half_solve, left_side=True, lower=True, transpose_a=True
    )[:, 0]
    update = jnp.dot(
        output_change_matrix[0],
        coefficients,
        precision=lax.Precision.HIGHEST,
        preferred_element_type=jnp.float32,
    )
    updated_interface_guess = tilde + update
    total_rows = rows_dev * lax.axis_size("slab") * lax.axis_size("wide")
    scaled = lax.linalg.triangular_solve(
        lower_factor, panel, left_side=False, lower=True, transpose_a=True
    )
    unitary_basis_factor = math.sqrt(total_rows) * scaled
    return (
        subdomain_thermal_state[None],
        updated_interface_guess[None],
        unitary_basis_factor[None],
    )


def solution(mesh):
    return jax.shard_map(
        shards,
        mesh=mesh,
        in_specs=(
            P("wide", "slab", None, None),
            P("wide", "slab", None, None),
            P(None, "wide", "slab", None, None),
            P("wide", "slab"),
            P("wide", "slab"),
            P("wide", "slab", None),
            P("wide", "slab", None),
        ),
        out_specs=(P("wide", "slab", None, None), P("wide", "slab"), P("wide", "slab", None)),
        check_vma=False,
    )
```

```python
import math

import jax
import jax.numpy as jnp
from jax import lax
from jax.experimental import pallas as pl
from jax.experimental.pallas import tpu as pltpu
from jax.sharding import Mesh
from jax.sharding import PartitionSpec as P

INTERFACE_STRIP = 64
SWEEPS = 4
STEP_SIZE = 0.11
HALF = 16
LANES = 128
SUBS = 8
REACH = SWEEPS
COEF_REACH = SWEEPS - 1
FINE = 2
FIELDS = 4
SLOTS = REACH + FINE + FIELDS * COEF_REACH
HIGHEST = lax.Precision.HIGHEST
ANY = pl.BlockSpec(memory_space=pl.ANY)
WHOLE = pl.BlockSpec(memory_space=pltpu.VMEM)


def gather_sum(value, axes):
    count = lax.axis_size(axes)
    copies = jnp.broadcast_to(value[None], (count, *value.shape))
    return jnp.sum(lax.all_to_all(copies, axes, 0, 0, tiled=True), axis=0)


def start_all(copies):
    for copy in copies:
        copy.start()
    return copies


def wait_all(copies):
    for copy in copies:
        copy.wait()


def pack_kernel(
    state, spread, flow, ghost, right_hi, right_lo, left_hi, left_lo, planes, parts, rows, sems
):
    count = state.shape[0]
    started = []
    for side, hi, lo, first, coef_first in (
        (0, right_hi, right_lo, count - REACH, count - COEF_REACH),
        (1, left_hi, left_lo, 0, 0),
    ):
        for part, out in ((0, lo), (1, hi)):
            band = pl.ds(part * HALF, HALF)
            source = [spread.at[pl.ds(coef_first, COEF_REACH), band, :]]
            source += [flow.at[axis, pl.ds(coef_first, COEF_REACH), band, :] for axis in range(3)]
            for field in range(FIELDS):
                slot = REACH + FINE + field * COEF_REACH
                started.append(
                    pltpu.make_async_copy(
                        source[field],
                        out.at[pl.ds(slot, COEF_REACH)],
                        sems.at[side * 8 + part * 4 + field],
                    )
                )
    fetch = [
        pltpu.make_async_copy(state.at[pl.ds(count - REACH, REACH)], planes.at[0], sems.at[16]),
        pltpu.make_async_copy(state.at[pl.ds(0, REACH)], planes.at[1], sems.at[17]),
    ]
    start_all(fetch)
    start_all(started)
    wait_all(fetch)
    for side, fine_first in ((0, REACH - FINE), (1, 0)):
        for part in range(2):
            band = pl.ds(part * HALF, HALF)
            for plane in range(REACH):
                value = planes[side, plane, band, :]
                lead = value.astype(jnp.bfloat16)
                parts[side, part, plane] = lead
                if fine_first <= plane < fine_first + FINE:
                    rest = value - lead.astype(jnp.float32)
                    parts[side, part, REACH + plane - fine_first] = rest.astype(jnp.bfloat16)
    for side, first in ((0, count - COEF_REACH), (1, 0)):
        value = ghost[pl.ds(first, COEF_REACH), :]
        pieces = []
        for _ in range(3):
            lead = value.astype(jnp.bfloat16).astype(jnp.float32)
            pieces.append(lead)
            value = value - lead
        pad = jnp.zeros((HALF - 3 * COEF_REACH, value.shape[1]), jnp.float32)
        rows[side] = jnp.concatenate([*pieces, pad], axis=0).astype(jnp.bfloat16)
    push = []
    for side, hi, lo in ((0, right_hi, right_lo), (1, left_hi, left_lo)):
        for part, out in ((0, lo), (1, hi)):
            push.append(
                pltpu.make_async_copy(
                    parts.at[side, part],
                    out.at[pl.ds(0, REACH + FINE)],
                    sems.at[18 + 2 * side + part],
                )
            )
        push.append(pltpu.make_async_copy(rows.at[side], hi.at[SLOTS], sems.at[22 + side]))
    start_all(push)
    wait_all(push)
    wait_all(started)


def pack(state, spread, flow, ghost):
    depth = state.shape[2]
    upper = jax.ShapeDtypeStruct((SLOTS + 1, HALF, depth), jnp.bfloat16)
    lower = jax.ShapeDtypeStruct((SLOTS, HALF, depth), jnp.bfloat16)
    return pl.pallas_call(
        pack_kernel,
        out_shape=(upper, lower, upper, lower),
        in_specs=[ANY, ANY, ANY, WHOLE],
        out_specs=(ANY,) * 4,
        scratch_shapes=[
            pltpu.VMEM((2, REACH, *state.shape[1:]), jnp.float32),
            pltpu.VMEM((2, 2, REACH + FINE, HALF, depth), jnp.bfloat16),
            pltpu.VMEM((2, HALF, depth), jnp.bfloat16),
            pltpu.SemaphoreType.DMA((24,)),
        ],
        cost_estimate=pl.CostEstimate(flops=2_000_000, bytes_accessed=6_000_000, transcendentals=0),
        name="pack_edges",
    )(state, spread, flow, ghost)


def plane_update(below_x, centre, above_x, coefs, ghost_row, store, tile_count, lane_blocks):
    lane = lax.broadcasted_iota(jnp.int32, (SUBS, LANES), 1)
    sub = lax.broadcasted_iota(jnp.int32, (SUBS, LANES), 0)
    zero = jnp.zeros((SUBS, LANES), jnp.float32)
    kept = {}

    def once(kind, tile, block, make):
        if (kind, tile, block) not in kept:
            kept[kind, tile, block] = make()
        return kept[kind, tile, block]

    def tile_of(tile, block):
        return once("c", tile, block, lambda: centre(tile, block))

    def rolled(tile, block, shift, axis):
        return once(
            (shift, axis), tile, block, lambda: pltpu.roll(tile_of(tile, block), shift, axis)
        )

    for block in range(lane_blocks):
        for tile in range(tile_count):
            here = tile_of(tile, block)
            down = rolled(tile, block, 1, 1)
            carry = rolled(tile, block - 1, 1, 1) if block else zero
            minus_z = jnp.where(lane == 0, carry, down)
            up = rolled(tile, block, LANES - 1, 1)
            last = block + 1 == lane_blocks
            carry = zero if last else rolled(tile, block + 1, LANES - 1, 1)
            plus_z = jnp.where(lane == LANES - 1, carry, up)
            carry = rolled(tile - 1, block, 1, 0) if tile else zero
            minus_y = jnp.where(sub == 0, carry, rolled(tile, block, 1, 0))
            top = tile + 1 == tile_count
            carry = ghost_row(block) if top else rolled(tile + 1, block, SUBS - 1, 0)
            plus_y = jnp.where(sub == SUBS - 1, carry, rolled(tile, block, SUBS - 1, 0))
            plus_x, minus_x = above_x(tile, block), below_x(tile, block)
            rate, flow_x, flow_y, flow_z = (coefs(field, tile, block) for field in range(FIELDS))
            total = ((plus_x + minus_x) + (plus_y + minus_y)) + (plus_z + minus_z) - 6.0 * here
            carried = (
                flow_x * (plus_x - minus_x)
                + flow_y * (plus_y - minus_y)
                + flow_z * (plus_z - minus_z)
            )
            change = rate * total - 0.5 * carried
            store(tile, block, here + STEP_SIZE * change)


def sweep(source, target, coefs, ghost, first, stop, tiles, coef_tile):
    lane_blocks = source.shape[2] // LANES

    def body(plane, carry):
        def tile_at(which):
            return lambda tile, block: source[
                which, pl.ds(tile * SUBS, SUBS), pl.ds(block * LANES, LANES)
            ]

        kept = {}

        def coef(field, tile, block):
            pair = (tile + coef_tile) // 2
            if (field, pair, block) not in kept:
                both = coefs[
                    field, plane - 1, pl.ds(pair * HALF, HALF), pl.ds(block * LANES, LANES)
                ]
                kept[field, pair, block] = both.astype(jnp.float32)
            low = (tile + coef_tile) % 2 * SUBS
            return kept[field, pair, block][low : low + SUBS]

        def ghost_row(block):
            return jnp.broadcast_to(
                ghost[plane, :, pl.ds(block * LANES, LANES)], (SUBS, LANES)
            )

        def store(tile, block, value):
            target[plane, pl.ds(tile * SUBS, SUBS), pl.ds(block * LANES, LANES)] = value

        plane_update(
            tile_at(plane - 1),
            tile_at(plane),
            tile_at(plane + 1),
            coef,
            ghost_row,
            store,
            tiles,
            lane_blocks,
        )
        return carry

    lax.fori_loop(first, stop, body, 0)


def set_ghosts(ghost, from_left, from_right, rows):
    count = rows.shape[0]
    rows3 = rows[...]
    for plane in range(count):
        ghost[REACH + plane] = rows3[plane : plane + 1]
    for first, message in ((REACH - COEF_REACH, from_left), (REACH + count, from_right)):
        value = message[...].astype(jnp.float32)
        for plane in range(COEF_REACH):
            row = value[plane : plane + 1]
            for part in (1, 2):
                at = part * COEF_REACH + plane
                row = row + value[at : at + 1]
            ghost[first + plane] = row


def set_edges(grid, parts, count, first_row, rows):
    for side, first, fine_first in ((0, 0, REACH - FINE), (1, REACH + count, 0)):
        for plane in range(REACH):
            value = parts[side, plane, pl.ds(rows, HALF - rows), :].astype(jnp.float32)
            if fine_first <= plane < fine_first + FINE:
                rest = parts[side, REACH + plane - fine_first, pl.ds(rows, HALF - rows), :]
                value = value + rest.astype(jnp.float32)
            grid[first + plane, pl.ds(first_row, HALF - rows), :] = value


def coefficient_copies(coefs, left, right, part, band, count, sems, at):
    copies = []
    for side, message, first in ((0, left, 0), (1, right, COEF_REACH + count)):
        for field in range(FIELDS):
            copies.append(
                pltpu.make_async_copy(
                    message.at[pl.ds(REACH + FINE + field * COEF_REACH, COEF_REACH)],
                    coefs.at[field, pl.ds(first, COEF_REACH), band, :],
                    sems.at[at + side * FIELDS + field],
                )
            )
    return copies


def face_kernel(
    state, spread, flow, rows, left, right, face, grid, other, coefs, parts, tails, ghost, sems
):
    count, height = state.shape[0], state.shape[1]
    band = pl.ds(height - HALF, HALF)
    inner = pl.ds(COEF_REACH, count)
    copies = [
        pltpu.make_async_copy(
            state.at[:, pl.ds(height - SUBS, SUBS), :], grid.at[pl.ds(REACH, count)], sems.at[0]
        ),
        pltpu.make_async_copy(spread.at[:, band, :], coefs.at[0, inner], sems.at[1]),
        pltpu.make_async_copy(left.at[pl.ds(0, REACH + FINE)], parts.at[0], sems.at[2]),
        pltpu.make_async_copy(right.at[pl.ds(0, REACH + FINE)], parts.at[1], sems.at[3]),
        pltpu.make_async_copy(left.at[SLOTS], tails.at[0], sems.at[4]),
        pltpu.make_async_copy(right.at[SLOTS], tails.at[1], sems.at[5]),
    ]
    for axis in range(3):
        copies.append(
            pltpu.make_async_copy(
                flow.at[axis, :, band, :], coefs.at[1 + axis, inner], sems.at[6 + axis]
            )
        )
    copies += coefficient_copies(coefs, left, right, 1, pl.ds(0, HALF), count, sems, 9)
    start_all(copies)
    wait_all(copies)
    set_ghosts(ghost, tails.at[0], tails.at[1], rows)
    set_edges(grid, parts, count, 0, HALF - SUBS)
    pair = (grid, other)
    for step in range(SWEEPS):
        sweep(
            pair[step % 2],
            pair[(step + 1) % 2],
            coefs,
            ghost,
            step + 1,
            count + 2 * REACH - 1 - step,
            1,
            1,
        )
    last = pair[SWEEPS % 2]
    strips = state.shape[2] // INTERFACE_STRIP
    top = last[pl.ds(REACH, count), SUBS - 1, :]
    strip = lax.broadcasted_iota(jnp.int32, (state.shape[2], strips), 0) // INTERFACE_STRIP
    column = lax.broadcasted_iota(jnp.int32, (state.shape[2], strips), 1)
    member = jnp.where(strip == column, 1.0 / INTERFACE_STRIP, 0.0)
    face[...] = jnp.dot(top, member, precision=HIGHEST, preferred_element_type=jnp.float32)


def interface_face(state, spread, flow, rows, left, right):
    count, _, depth = state.shape
    extended = count + 2 * REACH
    return pl.pallas_call(
        face_kernel,
        out_shape=jax.ShapeDtypeStruct((count, depth // INTERFACE_STRIP), jnp.float32),
        in_specs=[ANY, ANY, ANY, WHOLE, ANY, ANY],
        out_specs=WHOLE,
        scratch_shapes=[
            pltpu.VMEM((extended, SUBS, depth), jnp.float32),
            pltpu.VMEM((extended, SUBS, depth), jnp.float32),
            pltpu.VMEM((FIELDS, extended - 2, HALF, depth), jnp.bfloat16),
            pltpu.VMEM((2, REACH + FINE, HALF, depth), jnp.bfloat16),
            pltpu.VMEM((2, HALF, depth), jnp.bfloat16),
            pltpu.VMEM((extended, 1, depth), jnp.float32),
            pltpu.SemaphoreType.DMA((17,)),
        ],
        cost_estimate=pl.CostEstimate(
            flops=20_000_000, bytes_accessed=6_000_000, transcendentals=0
        ),
        name="interface_face",
    )(state, spread, flow, rows, left, right)


def field_kernel(
    state,
    spread,
    flow,
    rows,
    left_hi,
    left_lo,
    right_hi,
    right_lo,
    out,
    grid,
    other,
    coefs,
    parts,
    tails,
    ghost,
    sems,
):
    count, height = state.shape[0], state.shape[1]
    inner = pl.ds(COEF_REACH, count)
    copies = [
        pltpu.make_async_copy(state, grid.at[pl.ds(REACH, count)], sems.at[0]),
        pltpu.make_async_copy(spread, coefs.at[0, inner], sems.at[1]),
        pltpu.make_async_copy(left_lo.at[pl.ds(0, REACH + FINE)], parts.at[0, 0], sems.at[2]),
        pltpu.make_async_copy(right_lo.at[pl.ds(0, REACH + FINE)], parts.at[0, 1], sems.at[3]),
        pltpu.make_async_copy(left_hi.at[pl.ds(0, REACH + FINE)], parts.at[1, 0], sems.at[4]),
        pltpu.make_async_copy(right_hi.at[pl.ds(0, REACH + FINE)], parts.at[1, 1], sems.at[5]),
        pltpu.make_async_copy(left_hi.at[SLOTS], tails.at[0], sems.at[6]),
        pltpu.make_async_copy(right_hi.at[SLOTS], tails.at[1], sems.at[7]),
    ]
    for axis in range(3):
        copies.append(
            pltpu.make_async_copy(flow.at[axis], coefs.at[1 + axis, inner], sems.at[8 + axis])
        )
    copies += coefficient_copies(coefs, left_lo, right_lo, 0, pl.ds(0, HALF), count, sems, 11)
    copies += coefficient_copies(coefs, left_hi, right_hi, 1, pl.ds(HALF, HALF), count, sems, 19)
    start_all(copies)
    wait_all(copies)
    set_ghosts(ghost, tails.at[0], tails.at[1], rows)
    for part in range(2):
        set_edges(grid, parts.at[part], count, part * HALF, 0)
    pair = (grid, other)
    for step in range(SWEEPS):
        sweep(
            pair[step % 2],
            pair[(step + 1) % 2],
            coefs,
            ghost,
            step + 1,
            count + 2 * REACH - 1 - step,
            height // SUBS,
            0,
        )
    done = pltpu.make_async_copy(pair[SWEEPS % 2].at[pl.ds(REACH, count)], out, sems.at[0])
    done.start()
    done.wait()


def field(state, spread, flow, rows, left_hi, left_lo, right_hi, right_lo):
    count, height, depth = state.shape
    extended = count + 2 * REACH
    return pl.pallas_call(
        field_kernel,
        out_shape=jax.ShapeDtypeStruct(state.shape, jnp.float32),
        in_specs=[ANY, ANY, ANY, WHOLE, ANY, ANY, ANY, ANY],
        out_specs=ANY,
        scratch_shapes=[
            pltpu.VMEM((extended, height, depth), jnp.float32),
            pltpu.VMEM((extended, height, depth), jnp.float32),
            pltpu.VMEM((FIELDS, extended - 2, height, depth), jnp.bfloat16),
            pltpu.VMEM((2, 2, REACH + FINE, HALF, depth), jnp.bfloat16),
            pltpu.VMEM((2, HALF, depth), jnp.bfloat16),
            pltpu.VMEM((extended, 1, depth), jnp.float32),
            pltpu.SemaphoreType.DMA((27,)),
        ],
        compiler_params=pltpu.CompilerParams(vmem_limit_bytes=40 * 2**20),
        cost_estimate=pl.CostEstimate(
            flops=80_000_000, bytes_accessed=30_000_000, transcendentals=0
        ),
        name="field",
    )(state, spread, flow, rows, left_hi, left_lo, right_hi, right_lo)


def tilde_kernel(faces, partner_rows, guess, panel, tilde, projection):
    strips = faces.shape[1]
    wanted = partner_rows[...]
    line = lax.broadcasted_iota(jnp.int32, (faces.shape[0], wanted.shape[1]), 0)
    chosen = jnp.where(line == wanted // strips, 1.0, 0.0)
    picked = lax.dot_general(
        faces[...],
        chosen,
        (((0,), (0,)), ((), ())),
        precision=HIGHEST,
        preferred_element_type=jnp.float32,
    )
    spot = lax.broadcasted_iota(jnp.int32, picked.shape, 0)
    values = jnp.sum(jnp.where(spot == wanted % strips, picked, 0.0), axis=0, keepdims=True)
    tilde[...] = values
    projection[...] = jnp.dot(
        values - guess[...],
        panel[...],
        precision=HIGHEST,
        preferred_element_type=jnp.float32,
    )


def tilde_and_projection(faces, partner_rows, guess, panel):
    return pl.pallas_call(
        tilde_kernel,
        out_shape=(
            jax.ShapeDtypeStruct(guess.shape, jnp.float32),
            jax.ShapeDtypeStruct((1, panel.shape[1]), jnp.float32),
        ),
        in_specs=[WHOLE] * 4,
        out_specs=(WHOLE,) * 2,
        cost_estimate=pl.CostEstimate(flops=9_000_000, bytes_accessed=200_000, transcendentals=0),
        name="tilde",
    )(faces, partner_rows, guess, panel)


def shards(
    thermal_state,
    thermal_spreading_rate,
    flow_speed_vector,
    interface_guess,
    partner_facing_rows,
    mismatch_change_matrix,
    output_change_matrix,
):
    state = thermal_state[0]
    spread = thermal_spreading_rate[0]
    flow = flow_speed_vector[:, 0]
    panel = mismatch_change_matrix[0]
    layers = state.shape[0]
    slabs = lax.axis_size("slab")
    rows = jnp.repeat(interface_guess[0].reshape(layers, -1), INTERFACE_STRIP, axis=1)

    gram_local = lax.dot_general(
        panel,
        panel,
        (((0,), (0,)), ((), ())),
        precision=HIGHEST,
        preferred_element_type=jnp.float32,
    )
    blocks = gram_local.reshape(slabs, -1, gram_local.shape[1])
    gram_rows = jnp.sum(lax.all_to_all(blocks, "slab", 0, 0, tiled=True), axis=0)

    right_hi, right_lo, left_hi, left_lo = pack(state, spread, flow, rows)
    onward = [(i, i + 1) for i in range(slabs - 1)]
    back = [(i + 1, i) for i in range(slabs - 1)]
    from_left_hi = lax.ppermute(right_hi, "slab", onward)
    from_right_hi = lax.ppermute(left_hi, "slab", back)
    from_left_lo = lax.ppermute(right_lo, "slab", onward)
    from_right_lo = lax.ppermute(left_lo, "slab", back)
    face = interface_face(state, spread, flow, rows, from_left_hi, from_right_hi)

    both = 2 * slabs
    faces = lax.all_to_all(
        jnp.broadcast_to(face[None], (both, *face.shape)), ("half", "slab"), 0, 0, tiled=True
    )
    other = slabs * (1 - lax.axis_index("half"))
    faces = lax.dynamic_slice_in_dim(faces, other, slabs, axis=0).reshape(-1, face.shape[1])
    tilde, proj_local = tilde_and_projection(faces, partner_facing_rows, interface_guess, panel)

    gram_rows = gather_sum(gram_rows, ("half", "pair"))
    copies = jnp.broadcast_to(gram_rows[None], blocks.shape)
    gram_matrix = lax.all_to_all(copies, "slab", 0, 0, tiled=True).reshape(gram_local.shape)
    projection = gather_sum(proj_local[0], ("half", "pair", "slab"))
    temperature = field(
        state, spread, flow, rows, from_left_hi, from_left_lo, from_right_hi, from_right_lo
    )

    lower_factor = jnp.linalg.cholesky(gram_matrix)
    half_solve = lax.linalg.triangular_solve(
        lower_factor, projection[:, None], left_side=True, lower=True
    )
    coefficients = -lax.linalg.triangular_solve(
        lower_factor, half_solve, left_side=True, lower=True, transpose_a=True
    )[:, 0]
    update = jnp.dot(
        output_change_matrix[0],
        coefficients,
        precision=HIGHEST,
        preferred_element_type=jnp.float32,
    )
    total_rows = (
        interface_guess.shape[1] * slabs * lax.axis_size("half") * lax.axis_size("pair")
    )
    scaled = lax.linalg.triangular_solve(
        lower_factor, panel, left_side=False, lower=True, transpose_a=True
    )
    return (
        temperature[None],
        tilde + update[None],
        (math.sqrt(total_rows) * scaled)[None],
    )


def solution(mesh):
    wide, slab = mesh.shape["wide"], mesh.shape["slab"]
    fine = Mesh(mesh.devices.reshape(2, wide // 2, slab), ("half", "pair", "slab"))
    parts = ("half", "pair")
    return jax.shard_map(
        shards,
        mesh=fine,
        in_specs=(
            P(parts, "slab", None, None),
            P(parts, "slab", None, None),
            P(None, parts, "slab", None, None),
            P(parts, "slab"),
            P(parts, "slab"),
            P(parts, "slab", None),
            P(parts, "slab", None),
        ),
        out_specs=(P(parts, "slab", None, None), P(parts, "slab"), P(parts, "slab", None)),
        check_vma=False,
    )
```

```python
import functools
import math

import jax
import jax.numpy as jnp
from jax import lax
from jax.experimental import pallas as pl
from jax.experimental.pallas import tpu as pltpu
from jax.sharding import Mesh
from jax.sharding import PartitionSpec as P

INTERFACE_STRIP = 64
SWEEPS = 4
STEP_SIZE = 0.11
HALF = 16
LANES = 128
SUBS = 8
REACH = SWEEPS
COEF_REACH = SWEEPS - 1
FINE = 2
FIELDS = 4
SLOTS = REACH + FINE + FIELDS * COEF_REACH
HIGHEST = lax.Precision.HIGHEST
ANY = pl.BlockSpec(memory_space=pl.ANY)
WHOLE = pl.BlockSpec(memory_space=pltpu.VMEM)
SMALL = pltpu.CompilerParams(vmem_limit_bytes=8 * 2**20)
SCALARS = pl.BlockSpec(memory_space=pltpu.SMEM)


def start_all(copies):
    for copy in copies:
        copy.start()


def wait_all(copies):
    for copy in copies:
        copy.wait()


def ghost_line(guess, first, block):
    lane = lax.broadcasted_iota(jnp.int32, (1, LANES), 1)
    strips = LANES // INTERFACE_STRIP
    at = first + block * strips
    row = jnp.full((1, LANES), guess[0, at], jnp.float32)
    for strip in range(1, strips):
        row = jnp.where(lane < strip * INTERFACE_STRIP, row, guess[0, at + strip])
    return row


def pack_kernel(state, spread, flow, guess, right_hi, right_lo, left_hi, left_lo, planes, sems):
    count = state.shape[0]
    lane_blocks = state.shape[2] // LANES
    per_plane = guess.shape[1] // count
    fetch = [
        pltpu.make_async_copy(state.at[pl.ds(count - REACH, REACH)], planes.at[0], sems.at[16]),
        pltpu.make_async_copy(state.at[pl.ds(0, REACH)], planes.at[1], sems.at[17]),
    ]
    started = []
    for side, hi, lo, coef_first in (
        (0, right_hi, right_lo, count - COEF_REACH),
        (1, left_hi, left_lo, 0),
    ):
        for part, out in ((1, hi), (0, lo)):
            band = pl.ds(part * HALF, HALF)
            source = [spread.at[pl.ds(coef_first, COEF_REACH), band, :]]
            source += [flow.at[axis, pl.ds(coef_first, COEF_REACH), band, :] for axis in range(3)]
            for field in range(FIELDS):
                slot = REACH + FINE + field * COEF_REACH
                started.append(
                    pltpu.make_async_copy(
                        source[field],
                        out.at[pl.ds(slot, COEF_REACH)],
                        sems.at[side * 8 + part * 4 + field],
                    )
                )
    start_all(fetch)
    start_all(started)
    for side, out, first in ((0, right_hi, count - COEF_REACH), (1, left_hi, 0)):
        for block in range(lane_blocks):
            lines = [
                ghost_line(guess, (first + plane) * per_plane, block)
                for plane in range(COEF_REACH)
            ]
            pieces = []
            for _ in range(3):
                leads = [line.astype(jnp.bfloat16).astype(jnp.float32) for line in lines]
                lines = [line - lead for line, lead in zip(lines, leads)]
                pieces += leads
            pad = jnp.zeros((HALF - 3 * COEF_REACH, LANES), jnp.float32)
            whole = jnp.concatenate([*pieces, pad], axis=0).astype(jnp.bfloat16)
            out[SLOTS, :, pl.ds(block * LANES, LANES)] = whole
    wait_all(fetch)
    for side, outs, fine_first in (
        (0, (right_lo, right_hi), REACH - FINE),
        (1, (left_lo, left_hi), 0),
    ):
        for part, out in enumerate(outs):
            for plane in range(REACH):
                value = planes[side, plane, pl.ds(part * HALF, HALF), :]
                lead = value.astype(jnp.bfloat16)
                out[plane] = lead
                if fine_first <= plane < fine_first + FINE:
                    rest = value - lead.astype(jnp.float32)
                    out[REACH + plane - fine_first] = rest.astype(jnp.bfloat16)
    wait_all(started)


def pack(state, spread, flow, guess):
    depth = state.shape[2]
    upper = jax.ShapeDtypeStruct((SLOTS + 1, HALF, depth), jnp.bfloat16)
    lower = jax.ShapeDtypeStruct((SLOTS, HALF, depth), jnp.bfloat16)
    return pl.pallas_call(
        pack_kernel,
        out_shape=(upper, lower, upper, lower),
        in_specs=[ANY, ANY, ANY, SCALARS],
        out_specs=(WHOLE,) * 4,
        scratch_shapes=[
            pltpu.VMEM((2, REACH, *state.shape[1:]), jnp.float32),
            pltpu.SemaphoreType.DMA((18,)),
        ],
        cost_estimate=pl.CostEstimate(flops=2_000_000, bytes_accessed=6_000_000, transcendentals=0),
        compiler_params=pltpu.CompilerParams(vmem_limit_bytes=16 * 2**20),
        name="pack_edges",
    )(state, spread, flow, guess)


def weights_of(rate, flow_x, flow_y, flow_z):
    rate = STEP_SIZE * rate
    flow_x, flow_y, flow_z = (0.5 * STEP_SIZE * flow for flow in (flow_x, flow_y, flow_z))
    return (
        rate + flow_x,
        rate - flow_x,
        rate + flow_y,
        rate - flow_y,
        rate + flow_z,
        rate - flow_z,
        1.0 - 6.0 * rate,
    )


def plane_update(below_x, centre, above_x, weights, ghost_row, store, tile_count, lane_blocks):
    lane = lax.broadcasted_iota(jnp.int32, (SUBS, LANES), 1)
    sub = lax.broadcasted_iota(jnp.int32, (SUBS, LANES), 0)
    zero = jnp.zeros((SUBS, LANES), jnp.float32)
    kept = {}

    def rolled(tile, block, shift, axis):
        key = (tile, block, shift, axis)
        if key not in kept:
            kept[key] = pltpu.roll(centre(tile, block), shift, axis)
        return kept[key]

    for block in range(lane_blocks):
        for tile in range(tile_count):
            carry = rolled(tile, block - 1, 1, 1) if block else zero
            minus_z = jnp.where(lane == 0, carry, rolled(tile, block, 1, 1))
            last = block + 1 == lane_blocks
            carry = zero if last else rolled(tile, block + 1, LANES - 1, 1)
            plus_z = jnp.where(lane == LANES - 1, carry, rolled(tile, block, LANES - 1, 1))
            carry = rolled(tile - 1, block, 1, 0) if tile else zero
            minus_y = jnp.where(sub == 0, carry, rolled(tile, block, 1, 0))
            top = tile + 1 == tile_count
            carry = ghost_row(block) if top else rolled(tile + 1, block, SUBS - 1, 0)
            plus_y = jnp.where(sub == SUBS - 1, carry, rolled(tile, block, SUBS - 1, 0))
            weight = weights(tile, block)
            minus_x, plus_x, here = below_x(tile, block), above_x(tile, block), centre(tile, block)
            if len(weight) == FIELDS:
                rate, flow_x, flow_y, flow_z = weight
                total = ((plus_x + minus_x) + (plus_y + minus_y)) + (plus_z + minus_z)
                carried = (
                    flow_x * (plus_x - minus_x)
                    + flow_y * (plus_y - minus_y)
                    + flow_z * (plus_z - minus_z)
                )
                change = rate * (total - 6.0 * here) - 0.5 * carried
                store(tile, block, here + STEP_SIZE * change)
                continue
            total_x = weight[0] * minus_x + weight[1] * plus_x
            total_y = weight[2] * minus_y + weight[3] * plus_y
            total_z = weight[4] * minus_z + weight[5] * plus_z
            store(tile, block, (total_x + total_y) + (total_z + weight[6] * here))


def sweep(source, target, coefs, held, ghost, first, stop, tiles, coef_tile, unroll):
    lane_blocks = source.shape[2] // LANES

    def one(plane):
        def tile_at(which):
            loaded = {}

            def load(tile, block):
                if (tile, block) not in loaded:
                    loaded[tile, block] = source[
                        which, pl.ds(tile * SUBS, SUBS), pl.ds(block * LANES, LANES)
                    ]
                return loaded[tile, block]

            return load

        pairs = {}

        def coef(field, tile, block):
            pair = (tile + coef_tile) // 2
            if (field, pair, block) not in pairs:
                both = coefs[
                    field, plane - 1, pl.ds(pair * HALF, HALF), pl.ds(block * LANES, LANES)
                ]
                pairs[field, pair, block] = both.astype(jnp.float32)
            low = (tile + coef_tile) % 2 * SUBS
            return pairs[field, pair, block][low : low + SUBS]

        def weights(tile, block):
            spot = (plane - 1, pl.ds(tile * SUBS, SUBS), pl.ds(block * LANES, LANES))
            if coefs is None:
                return [held[index, *spot] for index in range(held.shape[0])]
            fields = [coef(field, tile, block) for field in range(FIELDS)]
            if held is None:
                return fields
            values = weights_of(*fields)
            for index, value in enumerate(values):
                held[index, *spot] = value
            return values

        def ghost_row(block):
            return jnp.broadcast_to(
                ghost[plane, :, pl.ds(block * LANES, LANES)], (SUBS, LANES)
            )

        def store(tile, block, value):
            target[plane, pl.ds(tile * SUBS, SUBS), pl.ds(block * LANES, LANES)] = value

        plane_update(
            tile_at(plane - 1),
            tile_at(plane),
            tile_at(plane + 1),
            weights,
            ghost_row,
            store,
            tiles,
            lane_blocks,
        )

    def body(step, carry):
        for inner in range(unroll):
            one(first + step * unroll + inner)
        return carry

    assert (stop - first) % unroll == 0
    lax.fori_loop(0, (stop - first) // unroll, body, 0)


def set_ghosts(ghost, from_left, from_right, guess, count):
    per_plane = guess.shape[1] // count
    for plane in range(count):
        for block in range(ghost.shape[2] // LANES):
            line = ghost_line(guess, plane * per_plane, block)
            ghost[REACH + plane, :, pl.ds(block * LANES, LANES)] = line
    for first, message in ((REACH - COEF_REACH, from_left), (REACH + count, from_right)):
        value = message[...].astype(jnp.float32)
        for plane in range(COEF_REACH):
            row = value[plane : plane + 1]
            for part in (1, 2):
                at = part * COEF_REACH + plane
                row = row + value[at : at + 1]
            ghost[first + plane] = row


def set_edges(grid, parts, count, first_row, rows):
    for side, first, fine_first in ((0, 0, REACH - FINE), (1, REACH + count, 0)):
        for plane in range(REACH):
            value = parts[side, plane, pl.ds(rows, HALF - rows), :].astype(jnp.float32)
            if fine_first <= plane < fine_first + FINE:
                rest = parts[side, REACH + plane - fine_first, pl.ds(rows, HALF - rows), :]
                value = value + rest.astype(jnp.float32)
            grid[first + plane, pl.ds(first_row, HALF - rows), :] = value


def coefficient_copies(coefs, left, right, part, band, count, sems, at):
    copies = []
    for side, message, first in ((0, left, 0), (1, right, COEF_REACH + count)):
        for field in range(FIELDS):
            copies.append(
                pltpu.make_async_copy(
                    message.at[pl.ds(REACH + FINE + field * COEF_REACH, COEF_REACH)],
                    coefs.at[field, pl.ds(first, COEF_REACH), band, :],
                    sems.at[at + side * FIELDS + field],
                )
            )
    return copies


def face_kernel(
    state, spread, flow, guess, left, right, face, grid, other, coefs, held, parts, tails, ghost, sems
):
    count, height = state.shape[0], state.shape[1]
    band = pl.ds(height - HALF, HALF)
    inner = pl.ds(COEF_REACH, count)
    copies = [
        pltpu.make_async_copy(
            state.at[:, pl.ds(height - SUBS, SUBS), :], grid.at[pl.ds(REACH, count)], sems.at[0]
        ),
        pltpu.make_async_copy(spread.at[:, band, :], coefs.at[0, inner], sems.at[1]),
        pltpu.make_async_copy(left.at[pl.ds(0, REACH + FINE)], parts.at[0], sems.at[2]),
        pltpu.make_async_copy(right.at[pl.ds(0, REACH + FINE)], parts.at[1], sems.at[3]),
        pltpu.make_async_copy(left.at[SLOTS], tails.at[0], sems.at[4]),
        pltpu.make_async_copy(right.at[SLOTS], tails.at[1], sems.at[5]),
    ]
    for axis in range(3):
        copies.append(
            pltpu.make_async_copy(
                flow.at[axis, :, band, :], coefs.at[1 + axis, inner], sems.at[6 + axis]
            )
        )
    copies += coefficient_copies(coefs, left, right, 1, pl.ds(0, HALF), count, sems, 9)
    start_all(copies)
    wait_all(copies)
    set_ghosts(ghost, tails.at[0], tails.at[1], guess, count)
    set_edges(grid, parts, count, 0, HALF - SUBS)
    pair = (grid, other)
    for step in range(SWEEPS):
        sweep(
            pair[step % 2],
            pair[(step + 1) % 2],
            None if step else coefs,
            held,
            ghost,
            step + 1,
            count + 2 * REACH - 1 - step,
            1,
            1,
            2,
        )
    last = pair[SWEEPS % 2]
    lane = lax.broadcasted_iota(jnp.int32, (count, LANES), 1)
    means = jnp.zeros((count, LANES), jnp.float32)
    strips = LANES // INTERFACE_STRIP
    for block in range(state.shape[2] // LANES):
        top = last[pl.ds(REACH, count), SUBS - 1, pl.ds(block * LANES, LANES)]
        for strip in range(strips):
            mine = (lane >= strip * INTERFACE_STRIP) & (lane < (strip + 1) * INTERFACE_STRIP)
            total = jnp.sum(jnp.where(mine, top, 0.0), axis=1, keepdims=True)
            means = jnp.where(lane == block * strips + strip, total / INTERFACE_STRIP, means)
    line = lax.broadcasted_iota(jnp.int32, (LANES, LANES), 0)
    column = lax.broadcasted_iota(jnp.int32, (LANES, LANES), 1)
    across = state.shape[2] // INTERFACE_STRIP
    spread_out = jnp.dot(
        means,
        jnp.where(column % across == line, 1.0, 0.0),
        precision=HIGHEST,
        preferred_element_type=jnp.float32,
    )
    per_row = LANES // across
    plane = lax.broadcasted_iota(jnp.int32, (per_row, LANES), 0)
    spot = lax.broadcasted_iota(jnp.int32, (per_row, LANES), 1) // across
    for row in range(face.shape[0]):
        mine = spread_out[row * per_row : (row + 1) * per_row]
        face[row] = jnp.sum(jnp.where(plane == spot, mine, 0.0), axis=0)


def interface_face(state, spread, flow, guess, left, right):
    count, _, depth = state.shape
    extended = count + 2 * REACH
    return pl.pallas_call(
        face_kernel,
        out_shape=jax.ShapeDtypeStruct((guess.shape[1] // LANES, LANES), jnp.float32),
        in_specs=[ANY, ANY, ANY, SCALARS, ANY, ANY],
        out_specs=WHOLE,
        scratch_shapes=[
            pltpu.VMEM((extended, SUBS, depth), jnp.float32),
            pltpu.VMEM((extended, SUBS, depth), jnp.float32),
            pltpu.VMEM((FIELDS, extended - 2, HALF, depth), jnp.bfloat16),
            pltpu.VMEM((2 * FIELDS - 1, extended - 2, SUBS, depth), jnp.float32),
            pltpu.VMEM((2, REACH + FINE, HALF, depth), jnp.bfloat16),
            pltpu.VMEM((2, HALF, depth), jnp.bfloat16),
            pltpu.VMEM((extended, 1, depth), jnp.float32),
            pltpu.SemaphoreType.DMA((17,)),
        ],
        cost_estimate=pl.CostEstimate(
            flops=20_000_000, bytes_accessed=6_000_000, transcendentals=0
        ),
        compiler_params=pltpu.CompilerParams(vmem_limit_bytes=16 * 2**20),
        name="interface_face",
    )(state, spread, flow, guess, left, right)


def field_kernel(
    state,
    spread,
    flow,
    guess,
    left_hi,
    left_lo,
    right_hi,
    right_lo,
    out,
    grid,
    other,
    coefs,
    parts,
    tails,
    ghost,
    sems,
):
    count, height = state.shape[0], state.shape[1]
    inner = pl.ds(COEF_REACH, count)
    copies = [
        pltpu.make_async_copy(state, grid.at[pl.ds(REACH, count)], sems.at[0]),
        pltpu.make_async_copy(spread, coefs.at[0, inner], sems.at[1]),
        pltpu.make_async_copy(left_lo.at[pl.ds(0, REACH + FINE)], parts.at[0, 0], sems.at[2]),
        pltpu.make_async_copy(right_lo.at[pl.ds(0, REACH + FINE)], parts.at[0, 1], sems.at[3]),
        pltpu.make_async_copy(left_hi.at[pl.ds(0, REACH + FINE)], parts.at[1, 0], sems.at[4]),
        pltpu.make_async_copy(right_hi.at[pl.ds(0, REACH + FINE)], parts.at[1, 1], sems.at[5]),
        pltpu.make_async_copy(left_hi.at[SLOTS], tails.at[0], sems.at[6]),
        pltpu.make_async_copy(right_hi.at[SLOTS], tails.at[1], sems.at[7]),
    ]
    for axis in range(3):
        copies.append(
            pltpu.make_async_copy(flow.at[axis], coefs.at[1 + axis, inner], sems.at[8 + axis])
        )
    copies += coefficient_copies(coefs, left_lo, right_lo, 0, pl.ds(0, HALF), count, sems, 11)
    copies += coefficient_copies(coefs, left_hi, right_hi, 1, pl.ds(HALF, HALF), count, sems, 19)
    start_all(copies)
    wait_all(copies)
    set_ghosts(ghost, tails.at[0], tails.at[1], guess, count)
    for part in range(2):
        set_edges(grid, parts.at[part], count, part * HALF, 0)
    pair = (grid, other)
    for step in range(SWEEPS):
        sweep(
            pair[step % 2],
            pair[(step + 1) % 2],
            coefs,
            None,
            ghost,
            step + 1,
            count + 2 * REACH - 1 - step,
            height // SUBS,
            0,
            1,
        )
    done = pltpu.make_async_copy(pair[SWEEPS % 2].at[pl.ds(REACH, count)], out, sems.at[0])
    done.start()
    done.wait()


def field(state, spread, flow, guess, left_hi, left_lo, right_hi, right_lo):
    count, height, depth = state.shape
    extended = count + 2 * REACH
    return pl.pallas_call(
        field_kernel,
        out_shape=jax.ShapeDtypeStruct(state.shape, jnp.float32),
        in_specs=[ANY, ANY, ANY, SCALARS, ANY, ANY, ANY, ANY],
        out_specs=ANY,
        scratch_shapes=[
            pltpu.VMEM((extended, height, depth), jnp.float32),
            pltpu.VMEM((extended, height, depth), jnp.float32),
            pltpu.VMEM((FIELDS, extended - 2, height, depth), jnp.bfloat16),
            pltpu.VMEM((2, 2, REACH + FINE, HALF, depth), jnp.bfloat16),
            pltpu.VMEM((2, HALF, depth), jnp.bfloat16),
            pltpu.VMEM((extended, 1, depth), jnp.float32),
            pltpu.SemaphoreType.DMA((27,)),
        ],
        cost_estimate=pl.CostEstimate(
            flops=80_000_000, bytes_accessed=30_000_000, transcendentals=0
        ),
        compiler_params=pltpu.CompilerParams(vmem_limit_bytes=20 * 2**20),
        name="field",
    )(state, spread, flow, guess, left_hi, left_lo, right_hi, right_lo)


def gram_kernel(panel, gram):
    value = panel[...]
    gram[...] = lax.dot_general(
        value,
        value,
        (((0,), (0,)), ((), ())),
        precision=HIGHEST,
        preferred_element_type=jnp.float32,
    )


def local_gram(panel):
    columns = panel.shape[1]
    return pl.pallas_call(
        gram_kernel,
        out_shape=jax.ShapeDtypeStruct((columns, columns), jnp.float32),
        in_specs=[WHOLE],
        out_specs=WHOLE,
        compiler_params=SMALL,
        cost_estimate=pl.CostEstimate(flops=9_000_000, bytes_accessed=200_000, transcendentals=0),
        name="gram",
    )(panel)


def sum_kernel(parts, *rest):
    *extra, sent = rest
    total = jnp.sum(parts[...], axis=0)
    if extra:
        lines = extra[0][...]
        pad = jnp.zeros((SUBS - lines.shape[0], lines.shape[1]), jnp.float32)
        total = jnp.concatenate([total, lines, pad], axis=0)
    for copy in range(sent.shape[0]):
        sent[copy] = total


def sum_and_copy(name, receivers, parts, *extra):
    _, rows, columns = parts.shape
    rows += SUBS if extra else 0
    return pl.pallas_call(
        sum_kernel,
        out_shape=jax.ShapeDtypeStruct((receivers, rows, columns), jnp.float32),
        in_specs=[WHOLE] * (1 + len(extra)),
        out_specs=WHOLE,
        compiler_params=SMALL,
        cost_estimate=pl.CostEstimate(flops=100_000, bytes_accessed=500_000, transcendentals=0),
        name=name,
    )(parts, *extra)


def tilde_kernel(gathered, partner_rows, guess, panel, tilde, sent):
    lines = guess.shape[1] // LANES
    first = gathered.shape[1] - SUBS
    table = jnp.concatenate(
        [gathered[slab, pl.ds(first, lines), :] for slab in range(gathered.shape[0])], axis=0
    )
    wanted = partner_rows[...]
    line = lax.broadcasted_iota(jnp.int32, (table.shape[0], wanted.shape[1]), 0)
    chosen = jnp.where(line == wanted // LANES, 1.0, 0.0)
    picked = lax.dot_general(
        table,
        chosen,
        (((0,), (0,)), ((), ())),
        precision=HIGHEST,
        preferred_element_type=jnp.float32,
    )
    spot = lax.broadcasted_iota(jnp.int32, picked.shape, 0)
    values = jnp.sum(jnp.where(spot == wanted % LANES, picked, 0.0), axis=0, keepdims=True)
    tilde[...] = values
    projection = jnp.dot(
        values - guess[...],
        panel[...],
        precision=HIGHEST,
        preferred_element_type=jnp.float32,
    )
    sent[...] = jnp.broadcast_to(projection[None], sent.shape)


def tilde_and_projection(gathered, partner_rows, guess, panel, receivers):
    return pl.pallas_call(
        tilde_kernel,
        out_shape=(
            jax.ShapeDtypeStruct(guess.shape, jnp.float32),
            jax.ShapeDtypeStruct((receivers, 1, panel.shape[1]), jnp.float32),
        ),
        in_specs=[WHOLE] * 4,
        out_specs=(WHOLE,) * 2,
        compiler_params=SMALL,
        cost_estimate=pl.CostEstimate(flops=9_000_000, bytes_accessed=900_000, transcendentals=0),
        name="tilde",
    )(gathered, partner_rows, guess, panel)


def small_inverse(block):
    size = len(block)
    left = [list(row) for row in block]
    unit = [[None] * size for _ in range(size)]
    reciprocals = []
    for a in range(size):
        reciprocal = 1.0 / left[a][a]
        reciprocals.append(reciprocal)
        for row in range(a + 1, size):
            factor = left[row][a] * reciprocal
            for column in range(a + 1, row + 1):
                left[row][column] = left[row][column] - factor * left[column][a]
            for column in range(a):
                known = unit[row][column]
                change = factor * unit[a][column]
                unit[row][column] = -change if known is None else known - change
            unit[row][a] = -factor
    return unit, reciprocals


def column_of(entries):
    sub = lax.broadcasted_iota(jnp.int32, (SUBS, LANES), 0)
    column = jnp.zeros((SUBS, LANES), jnp.float32)
    for row, entry in enumerate(entries):
        if entry is not None:
            column = jnp.where(sub == row, entry, column)
    return column


def inverse_factor(tiles):
    shape = (SUBS, LANES)
    lane = lax.broadcasted_iota(jnp.int32, shape, 1)
    sub = lax.broadcasted_iota(jnp.int32, shape, 0)
    tiles = list(tiles)
    done = []
    for home in range(len(tiles)):
        first = home * SUBS
        columns = [
            [
                jnp.broadcast_to(tile[:, first + b : first + b + 1], shape)
                for b in range(SUBS)
            ]
            for tile in tiles[home:]
        ]
        block = [
            [jnp.broadcast_to(columns[0][b][a : a + 1], shape) for b in range(a + 1)]
            for a in range(SUBS)
        ]
        panel = (lane >= first) & (lane < first + SUBS)
        own = jnp.where(panel, jnp.where(lane - first == sub, 1.0, 0.0), tiles[home])
        lines = [jnp.broadcast_to(own[a : a + 1], shape) for a in range(SUBS)]
        unit, reciprocals = small_inverse(block)
        result = own
        for b in range(SUBS - 1):
            result = result + column_of([unit[a][b] for a in range(SUBS)]) * lines[b]
        roots = jnp.sqrt(column_of(reciprocals))
        done.append(jnp.where(lane <= sub + first, result, 0.0) * roots)
        if home + 1 == len(tiles):
            break
        answers = [
            jnp.broadcast_to(result[a : a + 1], shape) * reciprocals[a] for a in range(SUBS)
        ]
        for index in range(home + 1, len(tiles)):
            tile = jnp.where(panel, 0.0, tiles[index])
            raw = columns[index - home]
            parts = []
            for a in range(SUBS):
                factor = raw[a]
                for b in range(a):
                    factor = factor + unit[a][b] * raw[b]
                parts.append(factor * answers[a])
            while len(parts) > 1:
                parts = [one + two for one, two in zip(parts[::2], parts[1::2])]
            tiles[index] = tile - parts[0]
    return done


def factor_kernel(total_rows, gathered, panel, inverse_out, basis):
    slabs, rows, _ = gathered.shape
    tiles = [
        gathered[slab, pl.ds(first, SUBS), :]
        for slab in range(slabs)
        for first in range(0, rows - SUBS, SUBS)
    ]
    inverse = jnp.concatenate(inverse_factor(tiles), axis=0)
    inverse_out[...] = inverse
    basis[...] = lax.dot_general(
        panel[...],
        inverse * math.sqrt(total_rows),
        (((1,), (1,)), ((), ())),
        precision=HIGHEST,
        preferred_element_type=jnp.float32,
    )


def factor_and_basis(total_rows, gathered, panel):
    columns = panel.shape[1]
    return pl.pallas_call(
        functools.partial(factor_kernel, total_rows),
        out_shape=(
            jax.ShapeDtypeStruct((columns, columns), jnp.float32),
            jax.ShapeDtypeStruct(panel.shape, jnp.float32),
        ),
        in_specs=[WHOLE] * 2,
        out_specs=(WHOLE,) * 2,
        compiler_params=SMALL,
        cost_estimate=pl.CostEstimate(flops=30_000_000, bytes_accessed=9_000_000, transcendentals=0),
        name="factor",
    )(gathered, panel)


def update_kernel(parts, inverse, changes, tilde, guess):
    projection = jnp.sum(parts[...], axis=0)
    across = (((1,), (1,)), ((), ()))
    half = lax.dot_general(
        projection, inverse[...], across, precision=HIGHEST, preferred_element_type=jnp.float32
    )
    coefficients = -jnp.dot(
        half, inverse[...], precision=HIGHEST, preferred_element_type=jnp.float32
    )
    guess[...] = tilde[...] + lax.dot_general(
        coefficients,
        changes[...],
        across,
        precision=HIGHEST,
        preferred_element_type=jnp.float32,
    )


def update(parts, inverse, changes, tilde):
    return pl.pallas_call(
        update_kernel,
        out_shape=jax.ShapeDtypeStruct(tilde.shape, jnp.float32),
        in_specs=[WHOLE] * 4,
        out_specs=WHOLE,
        compiler_params=SMALL,
        cost_estimate=pl.CostEstimate(flops=9_000_000, bytes_accessed=400_000, transcendentals=0),
        name="update",
    )(parts, inverse, changes, tilde)


def shards(
    thermal_state,
    thermal_spreading_rate,
    flow_speed_vector,
    interface_guess,
    partner_facing_rows,
    mismatch_change_matrix,
    output_change_matrix,
):
    state = thermal_state[0]
    spread = thermal_spreading_rate[0]
    flow = flow_speed_vector[:, 0]
    panel = mismatch_change_matrix[0]
    state, spread, flow = (
        pltpu.with_memory_space_constraint(value, pltpu.HBM) for value in (state, spread, flow)
    )
    slabs = lax.axis_size("slab")
    wide = lax.axis_size("half") * lax.axis_size("pair")

    everyone = ("half", "pair", "slab")
    onward = [(i, i + 1) for i in range(slabs - 1)]
    back = [(i + 1, i) for i in range(slabs - 1)]

    gram = local_gram(panel).reshape(slabs, -1, panel.shape[1])
    gram, early_guess = lax.optimization_barrier((gram, interface_guess))
    right_hi, right_lo, left_hi, left_lo = pack(state, spread, flow, early_guess)
    gram_parts = lax.all_to_all(gram, "slab", 0, 0, tiled=True)
    from_left_hi = lax.ppermute(right_hi, "slab", onward)
    from_right_hi = lax.ppermute(left_hi, "slab", back)
    from_left_lo = lax.ppermute(right_lo, "slab", onward)
    from_right_lo = lax.ppermute(left_lo, "slab", back)
    gram_parts = lax.all_to_all(
        sum_and_copy("sum_slab", wide, gram_parts), ("half", "pair"), 0, 0, tiled=True
    )
    face = interface_face(state, spread, flow, interface_guess, from_left_hi, from_right_hi)
    face = lax.ppermute(face, "half", [(0, 1), (1, 0)])
    gathered = lax.all_to_all(
        sum_and_copy("sum_wide", slabs, gram_parts, face), "slab", 0, 0, tiled=True
    )
    tilde, share = tilde_and_projection(
        gathered, partner_facing_rows, interface_guess, panel, slabs * wide
    )
    share = lax.all_to_all(share, everyone, 0, 0, tiled=True)
    temperature = field(
        state,
        spread,
        flow,
        interface_guess,
        from_left_hi,
        from_left_lo,
        from_right_hi,
        from_right_lo,
    )
    inverse, basis = factor_and_basis(panel.shape[0] * slabs * wide, gathered, panel)
    updated = update(share, inverse, output_change_matrix[0], tilde)
    return temperature[None], updated, basis[None]


def solution(mesh):
    wide, slab = mesh.shape["wide"], mesh.shape["slab"]
    fine = Mesh(mesh.devices.reshape(2, wide // 2, slab), ("half", "pair", "slab"))
    parts = ("half", "pair")
    return jax.shard_map(
        shards,
        mesh=fine,
        in_specs=(
            P(parts, "slab", None, None),
            P(parts, "slab", None, None),
            P(None, parts, "slab", None, None),
            P(parts, "slab"),
            P(parts, "slab"),
            P(parts, "slab", None),
            P(parts, "slab", None),
        ),
        out_specs=(P(parts, "slab", None, None), P(parts, "slab"), P(parts, "slab", None)),
        check_vma=False,
    )
```

```python
import functools
import math

import jax
import jax.numpy as jnp
from jax import lax
from jax.experimental import pallas as pl
from jax.experimental.pallas import tpu as pltpu
from jax.sharding import Mesh
from jax.sharding import PartitionSpec as P

INTERFACE_STRIP = 64
SWEEPS = 4
STEP_SIZE = 0.11
PACKED = 16
LANES = 128
SUBS = 8
REACH = SWEEPS
COEF_REACH = SWEEPS - 1
FINE = 0
FIELDS = 4
SLOTS = REACH + FINE + FIELDS * COEF_REACH
HIGHEST = lax.Precision.HIGHEST
ANY = pl.BlockSpec(memory_space=pl.ANY)
WHOLE = pl.BlockSpec(memory_space=pltpu.VMEM)
SMALL = pltpu.CompilerParams(vmem_limit_bytes=8 * 2**20)
SCALARS = pl.BlockSpec(memory_space=pltpu.SMEM)


def start_all(copies):
    for copy in copies:
        copy.start()


def wait_all(copies):
    for copy in copies:
        copy.wait()


def ghost_line(guess, first, block):
    lane = lax.broadcasted_iota(jnp.int32, (1, LANES), 1)
    strips = LANES // INTERFACE_STRIP
    at = first + block * strips
    row = jnp.full((1, LANES), guess[0, at], jnp.float32)
    for strip in range(1, strips):
        row = jnp.where(lane < strip * INTERFACE_STRIP, row, guess[0, at + strip])
    return row


def pack_kernel(state, spread, flow, guess, right, left, planes, sems):
    count = state.shape[0]
    lane_blocks = state.shape[2] // LANES
    per_plane = guess.shape[1] // count
    fetch = [
        pltpu.make_async_copy(state.at[pl.ds(count - REACH, REACH)], planes.at[0], sems.at[8]),
        pltpu.make_async_copy(state.at[pl.ds(0, REACH)], planes.at[1], sems.at[9]),
    ]
    started = []
    for side, out, first in ((0, right, count - COEF_REACH), (1, left, 0)):
        source = [spread.at[pl.ds(first, COEF_REACH)]]
        source += [flow.at[axis, pl.ds(first, COEF_REACH)] for axis in range(3)]
        for field in range(FIELDS):
            slot = REACH + FINE + field * COEF_REACH
            started.append(
                pltpu.make_async_copy(
                    source[field],
                    out.at[pl.ds(slot, COEF_REACH)],
                    sems.at[side * FIELDS + field],
                )
            )
    start_all(fetch)
    start_all(started)
    for out, first in ((right, count - COEF_REACH), (left, 0)):
        for block in range(lane_blocks):
            lines = [
                ghost_line(guess, (first + plane) * per_plane, block)
                for plane in range(COEF_REACH)
            ]
            pieces = []
            for _ in range(3):
                leads = [line.astype(jnp.bfloat16).astype(jnp.float32) for line in lines]
                lines = [line - lead for line, lead in zip(lines, leads)]
                pieces += leads
            pad = jnp.zeros((PACKED - 3 * COEF_REACH, LANES), jnp.float32)
            whole = jnp.concatenate([*pieces, pad], axis=0).astype(jnp.bfloat16)
            out[SLOTS, pl.ds(0, PACKED), pl.ds(block * LANES, LANES)] = whole
        unused = state.shape[1] - PACKED
        out[SLOTS, pl.ds(PACKED, unused), :] = jnp.zeros((unused, state.shape[2]), jnp.bfloat16)
    wait_all(fetch)
    for side, out, fine_first in ((0, right, REACH - FINE), (1, left, 0)):
        for plane in range(REACH):
            value = planes[side, plane]
            lead = value.astype(jnp.bfloat16)
            out[plane] = lead
            if fine_first <= plane < fine_first + FINE:
                rest = value - lead.astype(jnp.float32)
                out[REACH + plane - fine_first] = rest.astype(jnp.bfloat16)
    wait_all(started)


def pack(state, spread, flow, guess):
    message = jax.ShapeDtypeStruct((SLOTS + 1, *state.shape[1:]), jnp.bfloat16)
    return pl.pallas_call(
        pack_kernel,
        out_shape=(message, message),
        in_specs=[ANY, ANY, ANY, SCALARS],
        out_specs=(WHOLE,) * 2,
        scratch_shapes=[
            pltpu.VMEM((2, REACH, *state.shape[1:]), jnp.float32),
            pltpu.SemaphoreType.DMA((10,)),
        ],
        compiler_params=pltpu.CompilerParams(vmem_limit_bytes=16 * 2**20),
        cost_estimate=pl.CostEstimate(flops=2_000_000, bytes_accessed=9_000_000, transcendentals=0),
        name="pack_edges",
    )(state, spread, flow, guess)


def weights_of(mode, rate, flow_x, flow_y, flow_z):
    rate = STEP_SIZE * rate
    flow_x, flow_y, flow_z = (0.5 * STEP_SIZE * flow for flow in (flow_x, flow_y, flow_z))
    if mode == 4:
        return rate, flow_x, flow_y, flow_z
    return (
        rate + flow_x,
        rate - flow_x,
        rate + flow_y,
        rate - flow_y,
        rate + flow_z,
        rate - flow_z,
        1.0 - 6.0 * rate,
    )


def swept(here, minus, plus, weight):
    if len(weight) == 4:
        total = ((plus[0] + minus[0]) + (plus[1] + minus[1])) + (plus[2] + minus[2])
        carried = (
            weight[1] * (plus[0] - minus[0])
            + weight[2] * (plus[1] - minus[1])
            + weight[3] * (plus[2] - minus[2])
        )
        return here + (weight[0] * (total - 6.0 * here) - carried)
    x, y, z = (
        weight[2 * axis] * minus[axis] + weight[2 * axis + 1] * plus[axis] for axis in range(3)
    )
    return (x + y) + (z + weight[6] * here)


FLOOR = 8
UNROLL = 2


def sweep(source, target, coefs, held, height, first, stop):
    lane_blocks = source.shape[1]
    lane = lax.broadcasted_iota(jnp.int32, (SUBS, LANES), 1)
    zero = jnp.zeros((SUBS, LANES), jnp.float32)

    def pair(step, carry):
        low = first + step * UNROLL
        kept = {}

        def load(offset, tile, block, shift=0):
            key = (offset, tile, block, shift)
            if key not in kept:
                rows = pl.ds(FLOOR + tile * SUBS + shift, SUBS)
                kept[key] = source[low + offset, block, rows, :]
            return kept[key]

        def rolled(offset, tile, block, shift):
            key = ("rolled", offset, tile, block, shift)
            if key not in kept:
                kept[key] = pltpu.roll(load(offset, tile, block), shift, 1)
            return kept[key]

        for block in range(lane_blocks):
            for tile in range(height // SUBS):
                for offset in range(UNROLL):
                    plane = low + offset
                    carry_in = rolled(offset, tile, block - 1, 1) if block else zero
                    minus_z = jnp.where(lane == 0, carry_in, rolled(offset, tile, block, 1))
                    last = block + 1 == lane_blocks
                    carry_in = zero if last else rolled(offset, tile, block + 1, LANES - 1)
                    moved = rolled(offset, tile, block, LANES - 1)
                    plus_z = jnp.where(lane == LANES - 1, carry_in, moved)
                    minus = (load(offset - 1, tile, block), load(offset, tile, block, -1), minus_z)
                    plus = (load(offset + 1, tile, block), load(offset, tile, block, 1), plus_z)
                    rows = pl.ds(tile * SUBS, SUBS)
                    if coefs is None:
                        weight = [
                            held[index, plane - 1, block, rows, :]
                            for index in range(held.shape[0])
                        ]
                    else:
                        half = tile * SUBS % PACKED
                        key = ("coef", offset, tile * SUBS // PACKED, block)
                        if key not in kept:
                            packed = pl.ds(tile * SUBS - half, PACKED)
                            lanes = pl.ds(block * LANES, LANES)
                            kept[key] = [
                                coefs[field, plane - 1, packed, lanes].astype(jnp.float32)
                                for field in range(FIELDS)
                            ]
                        mode = FIELDS if held is None else held.shape[0]
                        fields = [field[half : half + SUBS] for field in kept[key]]
                        weight = weights_of(mode, *fields)
                        if held is not None:
                            for index, value in enumerate(weight):
                                held[index, plane - 1, block, rows, :] = value
                    value = swept(load(offset, tile, block), minus, plus, weight)
                    if len(target.shape) == 4:
                        target[plane, block, pl.ds(FLOOR + tile * SUBS, SUBS), :] = value
                    else:
                        target[plane - REACH, rows, pl.ds(block * LANES, LANES)] = value
        return carry

    assert (stop - first) % UNROLL == 0
    lax.fori_loop(0, (stop - first) // UNROLL, pair, 0)


def set_rims(grids, guess, count, height):
    per_plane = guess.shape[1] // count
    for grid in grids:
        for block in range(grid.shape[1]):
            grid[:, block, pl.ds(0, FLOOR), :] = jnp.zeros(
                (grid.shape[0], FLOOR, LANES), jnp.float32
            )
    for plane in range(count):
        for block in range(grids[0].shape[1]):
            line = ghost_line(guess, plane * per_plane, block)
            for grid in grids:
                grid[REACH + plane, block, pl.ds(FLOOR + height, 1), :] = line


def set_edges(grids, parts, count, height):
    for side, first, fine_first in ((0, 0, REACH - FINE), (1, REACH + count, 0)):
        near = first + REACH - COEF_REACH if side == 0 else first
        for block in range(grids[0].shape[1]):
            lanes = pl.ds(block * LANES, LANES)
            for plane in range(REACH):
                value = parts[side, plane, :, lanes].astype(jnp.float32)
                if fine_first <= plane < fine_first + FINE:
                    rest = parts[side, REACH + plane - fine_first, :, lanes]
                    value = value + rest.astype(jnp.float32)
                grids[0][first + plane, block, pl.ds(FLOOR, height), :] = value
            tail = parts[side, REACH + FINE, pl.ds(0, PACKED), lanes].astype(jnp.float32)
            for plane in range(COEF_REACH):
                row = tail[plane : plane + 1]
                for part in (1, 2):
                    at = part * COEF_REACH + plane
                    row = row + tail[at : at + 1]
                for grid in grids:
                    grid[near + plane, block, pl.ds(FLOOR + height, 1), :] = row


def face_means(last, face, count, height):
    lane_blocks = last.shape[2] // LANES
    lane = lax.broadcasted_iota(jnp.int32, (count, LANES), 1)
    means = jnp.zeros((count, LANES), jnp.float32)
    strips = LANES // INTERFACE_STRIP
    for block in range(lane_blocks):
        top = last[:, height - 1, pl.ds(block * LANES, LANES)]
        for strip in range(strips):
            mine = (lane >= strip * INTERFACE_STRIP) & (lane < (strip + 1) * INTERFACE_STRIP)
            total = jnp.sum(jnp.where(mine, top, 0.0), axis=1, keepdims=True)
            means = jnp.where(lane == block * strips + strip, total / INTERFACE_STRIP, means)
    line = lax.broadcasted_iota(jnp.int32, (LANES, LANES), 0)
    column = lax.broadcasted_iota(jnp.int32, (LANES, LANES), 1)
    across = lane_blocks * strips
    spread_out = jnp.dot(
        means,
        jnp.where(column % across == line, 1.0, 0.0),
        precision=HIGHEST,
        preferred_element_type=jnp.float32,
    )
    per_row = LANES // across
    plane = lax.broadcasted_iota(jnp.int32, (per_row, LANES), 0)
    spot = lax.broadcasted_iota(jnp.int32, (per_row, LANES), 1) // across
    for row in range(face.shape[0]):
        mine = spread_out[row * per_row : (row + 1) * per_row]
        face[row] = jnp.sum(jnp.where(plane == spot, mine, 0.0), axis=0)


HELD = 4


def field_kernel(
    state, spread, flow, guess, left, right, out, face, grid, other, plain, coefs, parts, *rest
):
    *held, sems = rest
    held = held[0] if held else None
    count, height = state.shape[0], state.shape[1]
    lane_blocks = grid.shape[1]
    inner = pl.ds(COEF_REACH, count)
    parted = pl.ds(0, REACH + FINE)
    early = [
        pltpu.make_async_copy(state, plain, sems.at[0]),
        pltpu.make_async_copy(left.at[parted], parts.at[0, parted], sems.at[1]),
        pltpu.make_async_copy(right.at[parted], parts.at[1, parted], sems.at[2]),
        pltpu.make_async_copy(left.at[SLOTS], parts.at[0, REACH + FINE], sems.at[3]),
        pltpu.make_async_copy(right.at[SLOTS], parts.at[1, REACH + FINE], sems.at[4]),
    ]
    later = [pltpu.make_async_copy(spread, coefs.at[0, inner], sems.at[5])]
    for axis in range(3):
        later.append(
            pltpu.make_async_copy(flow.at[axis], coefs.at[1 + axis, inner], sems.at[6 + axis])
        )
    for side, message, first in ((0, left, 0), (1, right, COEF_REACH + count)):
        for field in range(FIELDS):
            later.append(
                pltpu.make_async_copy(
                    message.at[pl.ds(REACH + FINE + field * COEF_REACH, COEF_REACH)],
                    coefs.at[field, pl.ds(first, COEF_REACH)],
                    sems.at[9 + side * FIELDS + field],
                )
            )
    start_all(early)
    start_all(later)
    set_rims((grid, other), guess, count, height)
    wait_all(early)
    set_edges((grid, other), parts, count, height)
    for plane in range(count):
        for block in range(lane_blocks):
            grid[REACH + plane, block, pl.ds(FLOOR, height), :] = plain[
                plane, :, pl.ds(block * LANES, LANES)
            ]
    wait_all(later)
    pair = (grid, other)
    for step in range(SWEEPS - 1):
        sweep(
            pair[step % 2],
            pair[(step + 1) % 2],
            None if step and held is not None else coefs,
            held,
            height,
            step + 1,
            count + 2 * REACH - 1 - step,
        )
    pushes = []
    pieces = 2
    for piece in range(pieces):
        first = piece * count // pieces
        planes = pl.ds(first, count // pieces)
        sweep(
            pair[(SWEEPS - 1) % 2],
            plain,
            None if held is not None else coefs,
            held,
            height,
            REACH + first,
            REACH + first + count // pieces,
        )
        pushes.append(pltpu.make_async_copy(plain.at[planes], out.at[planes], sems.at[piece]))
        pushes[-1].start()
    face_means(plain, face, count, height)
    wait_all(pushes)


def field_and_face(state, spread, flow, guess, left, right):
    count, height, depth = state.shape
    extended = count + 2 * REACH
    lane_blocks = depth // LANES
    tall = FLOOR + height + SUBS
    held = [pltpu.VMEM((HELD, extended - 2, lane_blocks, height, LANES), jnp.float32)]
    return pl.pallas_call(
        field_kernel,
        out_shape=(
            jax.ShapeDtypeStruct(state.shape, jnp.float32),
            jax.ShapeDtypeStruct((guess.shape[1] // LANES, LANES), jnp.float32),
        ),
        in_specs=[ANY, ANY, ANY, SCALARS, ANY, ANY],
        out_specs=(pl.BlockSpec(memory_space=pltpu.HBM), WHOLE),
        scratch_shapes=[
            pltpu.VMEM((extended, lane_blocks, tall, LANES), jnp.float32),
            pltpu.VMEM((extended, lane_blocks, tall, LANES), jnp.float32),
            pltpu.VMEM(state.shape, jnp.float32),
            pltpu.VMEM((FIELDS, extended - 2, height, depth), jnp.bfloat16),
            pltpu.VMEM((2, REACH + FINE + 1, height, depth), jnp.bfloat16),
            *(held if HELD else []),
            pltpu.SemaphoreType.DMA((17,)),
        ],
        compiler_params=pltpu.CompilerParams(vmem_limit_bytes=(24 + 3 * HELD) * 2**20),
        cost_estimate=pl.CostEstimate(
            flops=80_000_000, bytes_accessed=30_000_000, transcendentals=0
        ),
        name="field",
    )(state, spread, flow, guess, left, right)


def gram_kernel(panel, gram):
    value = panel[...]
    gram[...] = lax.dot_general(
        value,
        value,
        (((0,), (0,)), ((), ())),
        precision=HIGHEST,
        preferred_element_type=jnp.float32,
    )


def local_gram(panel):
    columns = panel.shape[1]
    return pl.pallas_call(
        gram_kernel,
        out_shape=jax.ShapeDtypeStruct((columns, columns), jnp.float32),
        in_specs=[WHOLE],
        out_specs=WHOLE,
        compiler_params=SMALL,
        cost_estimate=pl.CostEstimate(flops=9_000_000, bytes_accessed=200_000, transcendentals=0),
        name="gram",
    )(panel)


def sum_kernel(parts, *rest):
    *extra, sent = rest
    total = jnp.sum(parts[...], axis=0)
    if extra:
        lines = extra[0][...]
        pad = jnp.zeros((SUBS - lines.shape[0], lines.shape[1]), jnp.float32)
        total = jnp.concatenate([total, lines, pad], axis=0)
    for copy in range(sent.shape[0]):
        sent[copy] = total


def sum_and_copy(name, receivers, parts, *extra):
    _, rows, columns = parts.shape
    rows += SUBS if extra else 0
    return pl.pallas_call(
        sum_kernel,
        out_shape=jax.ShapeDtypeStruct((receivers, rows, columns), jnp.float32),
        in_specs=[WHOLE] * (1 + len(extra)),
        out_specs=WHOLE,
        compiler_params=SMALL,
        cost_estimate=pl.CostEstimate(flops=100_000, bytes_accessed=500_000, transcendentals=0),
        name=name,
    )(parts, *extra)


def tilde_kernel(gathered, partner_rows, guess, panel, tilde, sent):
    lines = guess.shape[1] // LANES
    first = gathered.shape[1] - SUBS
    table = jnp.concatenate(
        [gathered[slab, pl.ds(first, lines), :] for slab in range(gathered.shape[0])], axis=0
    )
    wanted = partner_rows[...]
    line = lax.broadcasted_iota(jnp.int32, (table.shape[0], wanted.shape[1]), 0)
    chosen = jnp.where(line == wanted // LANES, 1.0, 0.0)
    picked = lax.dot_general(
        table,
        chosen,
        (((0,), (0,)), ((), ())),
        precision=HIGHEST,
        preferred_element_type=jnp.float32,
    )
    spot = lax.broadcasted_iota(jnp.int32, picked.shape, 0)
    values = jnp.sum(jnp.where(spot == wanted % LANES, picked, 0.0), axis=0, keepdims=True)
    tilde[...] = values
    projection = jnp.dot(
        values - guess[...],
        panel[...],
        precision=HIGHEST,
        preferred_element_type=jnp.float32,
    )
    sent[...] = jnp.broadcast_to(projection[None], sent.shape)


def tilde_and_projection(gathered, partner_rows, guess, panel, receivers):
    return pl.pallas_call(
        tilde_kernel,
        out_shape=(
            jax.ShapeDtypeStruct(guess.shape, jnp.float32),
            jax.ShapeDtypeStruct((receivers, 1, panel.shape[1]), jnp.float32),
        ),
        in_specs=[WHOLE] * 4,
        out_specs=(WHOLE,) * 2,
        compiler_params=SMALL,
        cost_estimate=pl.CostEstimate(flops=9_000_000, bytes_accessed=900_000, transcendentals=0),
        name="tilde",
    )(gathered, partner_rows, guess, panel)


def small_inverse(block):
    size = len(block)
    left = [list(row) for row in block]
    unit = [[None] * size for _ in range(size)]
    reciprocals = []
    for a in range(size):
        reciprocal = 1.0 / left[a][a]
        reciprocals.append(reciprocal)
        for row in range(a + 1, size):
            factor = left[row][a] * reciprocal
            for column in range(a + 1, row + 1):
                left[row][column] = left[row][column] - factor * left[column][a]
            for column in range(a):
                known = unit[row][column]
                change = factor * unit[a][column]
                unit[row][column] = -change if known is None else known - change
            unit[row][a] = -factor
    return unit, reciprocals


def column_of(entries):
    sub = lax.broadcasted_iota(jnp.int32, (SUBS, LANES), 0)
    column = jnp.zeros((SUBS, LANES), jnp.float32)
    for row, entry in enumerate(entries):
        if entry is not None:
            column = jnp.where(sub == row, entry, column)
    return column


def inverse_factor(tiles):
    shape = (SUBS, LANES)
    lane = lax.broadcasted_iota(jnp.int32, shape, 1)
    sub = lax.broadcasted_iota(jnp.int32, shape, 0)
    tiles = list(tiles)
    done = []
    for home in range(len(tiles)):
        first = home * SUBS
        columns = [
            [
                jnp.broadcast_to(tile[:, first + b : first + b + 1], shape)
                for b in range(SUBS)
            ]
            for tile in tiles[home:]
        ]
        block = [
            [jnp.broadcast_to(columns[0][b][a : a + 1], shape) for b in range(a + 1)]
            for a in range(SUBS)
        ]
        panel = (lane >= first) & (lane < first + SUBS)
        own = jnp.where(panel, jnp.where(lane - first == sub, 1.0, 0.0), tiles[home])
        lines = [jnp.broadcast_to(own[a : a + 1], shape) for a in range(SUBS)]
        unit, reciprocals = small_inverse(block)
        result = own
        for b in range(SUBS - 1):
            result = result + column_of([unit[a][b] for a in range(SUBS)]) * lines[b]
        roots = jnp.sqrt(column_of(reciprocals))
        done.append(jnp.where(lane <= sub + first, result, 0.0) * roots)
        if home + 1 == len(tiles):
            break
        answers = [
            jnp.broadcast_to(result[a : a + 1], shape) * reciprocals[a] for a in range(SUBS)
        ]
        for index in range(home + 1, len(tiles)):
            tile = jnp.where(panel, 0.0, tiles[index])
            raw = columns[index - home]
            parts = []
            for a in range(SUBS):
                factor = raw[a]
                for b in range(a):
                    factor = factor + unit[a][b] * raw[b]
                parts.append(factor * answers[a])
            while len(parts) > 1:
                parts = [one + two for one, two in zip(parts[::2], parts[1::2])]
            tiles[index] = tile - parts[0]
    return done


def factor_kernel(total_rows, gathered, panel, inverse_out, basis):
    slabs, rows, _ = gathered.shape
    tiles = [
        gathered[slab, pl.ds(first, SUBS), :]
        for slab in range(slabs)
        for first in range(0, rows - SUBS, SUBS)
    ]
    inverse = jnp.concatenate(inverse_factor(tiles), axis=0)
    inverse_out[...] = inverse
    basis[...] = lax.dot_general(
        panel[...],
        inverse * math.sqrt(total_rows),
        (((1,), (1,)), ((), ())),
        precision=HIGHEST,
        preferred_element_type=jnp.float32,
    )


def factor_and_basis(total_rows, gathered, panel):
    columns = panel.shape[1]
    return pl.pallas_call(
        functools.partial(factor_kernel, total_rows),
        out_shape=(
            jax.ShapeDtypeStruct((columns, columns), jnp.float32),
            jax.ShapeDtypeStruct(panel.shape, jnp.float32),
        ),
        in_specs=[WHOLE] * 2,
        out_specs=(WHOLE,) * 2,
        compiler_params=SMALL,
        cost_estimate=pl.CostEstimate(flops=30_000_000, bytes_accessed=9_000_000, transcendentals=0),
        name="factor",
    )(gathered, panel)


def update_kernel(parts, inverse, changes, tilde, guess):
    projection = jnp.sum(parts[...], axis=0)
    across = (((1,), (1,)), ((), ()))
    half = lax.dot_general(
        projection, inverse[...], across, precision=HIGHEST, preferred_element_type=jnp.float32
    )
    coefficients = -jnp.dot(
        half, inverse[...], precision=HIGHEST, preferred_element_type=jnp.float32
    )
    guess[...] = tilde[...] + lax.dot_general(
        coefficients,
        changes[...],
        across,
        precision=HIGHEST,
        preferred_element_type=jnp.float32,
    )


def update(parts, inverse, changes, tilde):
    return pl.pallas_call(
        update_kernel,
        out_shape=jax.ShapeDtypeStruct(tilde.shape, jnp.float32),
        in_specs=[WHOLE] * 4,
        out_specs=WHOLE,
        compiler_params=SMALL,
        cost_estimate=pl.CostEstimate(flops=9_000_000, bytes_accessed=400_000, transcendentals=0),
        name="update",
    )(parts, inverse, changes, tilde)


def shards(
    thermal_state,
    thermal_spreading_rate,
    flow_speed_vector,
    interface_guess,
    partner_facing_rows,
    mismatch_change_matrix,
    output_change_matrix,
):
    state = thermal_state[0]
    spread = thermal_spreading_rate[0]
    flow = flow_speed_vector[:, 0]
    panel = mismatch_change_matrix[0]
    state, spread, flow = (
        pltpu.with_memory_space_constraint(value, pltpu.HBM) for value in (state, spread, flow)
    )
    slabs = lax.axis_size("slab")
    wide = lax.axis_size("half") * lax.axis_size("pair")

    everyone = ("half", "pair", "slab")
    onward = [(i, i + 1) for i in range(slabs - 1)]
    back = [(i + 1, i) for i in range(slabs - 1)]

    gram = local_gram(panel).reshape(slabs, -1, panel.shape[1])
    gram, early_guess = lax.optimization_barrier((gram, interface_guess))
    right, left = pack(state, spread, flow, early_guess)
    gram_parts = lax.all_to_all(gram, "slab", 0, 0, tiled=True)
    right, left, gram_parts = lax.optimization_barrier((right, left, gram_parts))
    from_left = lax.ppermute(right, "slab", onward)
    from_right = lax.ppermute(left, "slab", back)
    gram_parts = lax.all_to_all(
        sum_and_copy("sum_slab", wide, gram_parts), ("half", "pair"), 0, 0, tiled=True
    )
    temperature, face = field_and_face(
        state, spread, flow, interface_guess, from_left, from_right
    )
    face = lax.ppermute(face, "half", [(0, 1), (1, 0)])
    gathered = lax.all_to_all(
        sum_and_copy("sum_wide", slabs, gram_parts, face), "slab", 0, 0, tiled=True
    )
    tilde, share = tilde_and_projection(
        gathered, partner_facing_rows, interface_guess, panel, slabs * wide
    )
    share = lax.all_to_all(share, everyone, 0, 0, tiled=True)
    inverse, basis = factor_and_basis(panel.shape[0] * slabs * wide, gathered, panel)
    updated = update(share, inverse, output_change_matrix[0], tilde)
    return temperature[None], updated, basis[None]


def solution(mesh):
    wide, slab = mesh.shape["wide"], mesh.shape["slab"]
    fine = Mesh(mesh.devices.reshape(2, wide // 2, slab), ("half", "pair", "slab"))
    parts = ("half", "pair")
    return jax.shard_map(
        shards,
        mesh=fine,
        in_specs=(
            P(parts, "slab", None, None),
            P(parts, "slab", None, None),
            P(None, parts, "slab", None, None),
            P(parts, "slab"),
            P(parts, "slab"),
            P(parts, "slab", None),
            P(parts, "slab", None),
        ),
        out_specs=(P(parts, "slab", None, None), P(parts, "slab"), P(parts, "slab", None)),
        check_vma=False,
    )
```

```python
import functools
import math

import jax
import jax.numpy as jnp
from jax import lax
from jax.experimental import pallas as pl
from jax.experimental.pallas import tpu as pltpu
from jax.sharding import Mesh
from jax.sharding import PartitionSpec as P

INTERFACE_STRIP = 64
SWEEPS = 4
STEP_SIZE = 0.11
PACKED = 16
LANES = 128
SUBS = 8
REACH = SWEEPS
COEF_REACH = SWEEPS - 1
FINE = 1
FIELDS = 4
SLOTS = REACH + FINE + FIELDS * COEF_REACH
HIGHEST = lax.Precision.HIGHEST
ANY = pl.BlockSpec(memory_space=pl.ANY)
WHOLE = pl.BlockSpec(memory_space=pltpu.VMEM)
SMALL = pltpu.CompilerParams(vmem_limit_bytes=8 * 2**20)
SCALARS = pl.BlockSpec(memory_space=pltpu.SMEM)


def start_all(copies):
    for copy in copies:
        copy.start()


def wait_all(copies):
    for copy in copies:
        copy.wait()


def ghost_line(guess, first, block):
    lane = lax.broadcasted_iota(jnp.int32, (1, LANES), 1)
    strips = LANES // INTERFACE_STRIP
    at = first + block * strips
    row = jnp.full((1, LANES), guess[0, at], jnp.float32)
    for strip in range(1, strips):
        row = jnp.where(lane < strip * INTERFACE_STRIP, row, guess[0, at + strip])
    return row


def pack_kernel(
    state, spread, flow, guess, right_out, left_out, right, left, planes, sems
):
    count = state.shape[0]
    lane_blocks = state.shape[2] // LANES
    per_plane = guess.shape[1] // count
    fetch = [
        pltpu.make_async_copy(state.at[pl.ds(count - REACH, REACH)], planes.at[0], sems.at[8]),
        pltpu.make_async_copy(state.at[pl.ds(0, REACH)], planes.at[1], sems.at[9]),
    ]
    started = []
    for side, out, first in ((0, right, count - COEF_REACH), (1, left, 0)):
        source = [spread.at[pl.ds(first, COEF_REACH)]]
        source += [flow.at[axis, pl.ds(first, COEF_REACH)] for axis in range(3)]
        for field in range(FIELDS):
            slot = REACH + FINE + field * COEF_REACH
            started.append(
                pltpu.make_async_copy(
                    source[field],
                    out.at[pl.ds(slot, COEF_REACH)],
                    sems.at[side * FIELDS + field],
                )
            )
    start_all(fetch)
    start_all(started)
    for out, first in ((right, count - COEF_REACH), (left, 0)):
        for block in range(lane_blocks):
            lines = [
                ghost_line(guess, (first + plane) * per_plane, block)
                for plane in range(COEF_REACH)
            ]
            pieces = []
            for _ in range(3):
                leads = [line.astype(jnp.bfloat16).astype(jnp.float32) for line in lines]
                lines = [line - lead for line, lead in zip(lines, leads)]
                pieces += leads
            pad = jnp.zeros((PACKED - 3 * COEF_REACH, LANES), jnp.float32)
            whole = jnp.concatenate([*pieces, pad], axis=0).astype(jnp.bfloat16)
            out[SLOTS, pl.ds(0, PACKED), pl.ds(block * LANES, LANES)] = whole
        unused = state.shape[1] - PACKED
        out[SLOTS, pl.ds(PACKED, unused), :] = jnp.zeros((unused, state.shape[2]), jnp.bfloat16)
    wait_all(fetch)
    for side, out, fine_first in ((0, right, REACH - FINE), (1, left, 0)):
        for plane in range(REACH):
            value = planes[side, plane]
            lead = value.astype(jnp.bfloat16)
            out[plane] = lead
            if fine_first <= plane < fine_first + FINE:
                rest = value - lead.astype(jnp.float32)
                out[REACH + plane - fine_first] = rest.astype(jnp.bfloat16)
    wait_all(started)
    pushes = [
        pltpu.make_async_copy(right, right_out, sems.at[8]),
        pltpu.make_async_copy(left, left_out, sems.at[9]),
    ]
    start_all(pushes)
    wait_all(pushes)


def pack(state, spread, flow, guess):
    message = jax.ShapeDtypeStruct((SLOTS + 1, *state.shape[1:]), jnp.bfloat16)
    return pl.pallas_call(
        pack_kernel,
        out_shape=(pltpu.HBM(message.shape, message.dtype),) * 2,
        in_specs=[ANY, ANY, ANY, SCALARS],
        out_specs=(pl.BlockSpec(memory_space=pltpu.HBM),) * 2,
        scratch_shapes=[
            pltpu.VMEM(message.shape, message.dtype),
            pltpu.VMEM(message.shape, message.dtype),
            pltpu.VMEM((2, REACH, *state.shape[1:]), jnp.float32),
            pltpu.SemaphoreType.DMA((10,)),
        ],
        compiler_params=pltpu.CompilerParams(vmem_limit_bytes=16 * 2**20),
        cost_estimate=pl.CostEstimate(flops=2_000_000, bytes_accessed=9_000_000, transcendentals=0),
        name="pack_edges",
    )(state, spread, flow, guess)


def weights_of(mode, rate, flow_x, flow_y, flow_z):
    rate = STEP_SIZE * rate
    flow_x, flow_y, flow_z = (0.5 * STEP_SIZE * flow for flow in (flow_x, flow_y, flow_z))
    if mode == 4:
        return rate, flow_x, flow_y, flow_z
    return (
        rate + flow_x,
        rate - flow_x,
        rate + flow_y,
        rate - flow_y,
        rate + flow_z,
        rate - flow_z,
        1.0 - 6.0 * rate,
    )


def swept(here, minus, plus, weight):
    if len(weight) == 4:
        total = ((plus[0] + minus[0]) + (plus[1] + minus[1])) + (plus[2] + minus[2])
        carried = (
            weight[1] * (plus[0] - minus[0])
            + weight[2] * (plus[1] - minus[1])
            + weight[3] * (plus[2] - minus[2])
        )
        return here + (weight[0] * (total - 6.0 * here) - carried)
    x, y, z = (
        weight[2 * axis] * minus[axis] + weight[2 * axis + 1] * plus[axis] for axis in range(3)
    )
    return (x + y) + (z + weight[6] * here)


FLOOR = 8
UNROLL = 2


def sweep(source, target, coefs, held, height, first, stop, shift=0):
    lane_blocks = source.shape[1]
    lane = lax.broadcasted_iota(jnp.int32, (SUBS, LANES), 1)
    zero = jnp.zeros((SUBS, LANES), jnp.float32)

    def pair(step, carry):
        low = first + step * UNROLL
        kept = {}

        def load(offset, tile, block, shift=0):
            key = (offset, tile, block, shift)
            if key not in kept:
                rows = pl.ds(FLOOR + tile * SUBS + shift, SUBS)
                kept[key] = source[low + offset, block, rows, :]
            return kept[key]

        def rolled(offset, tile, block, shift):
            key = ("rolled", offset, tile, block, shift)
            if key not in kept:
                kept[key] = pltpu.roll(load(offset, tile, block), shift, 1)
            return kept[key]

        for block in range(lane_blocks):
            for tile in range(height // SUBS):
                for offset in range(UNROLL):
                    plane = low + offset
                    carry_in = rolled(offset, tile, block - 1, 1) if block else zero
                    minus_z = jnp.where(lane == 0, carry_in, rolled(offset, tile, block, 1))
                    last = block + 1 == lane_blocks
                    carry_in = zero if last else rolled(offset, tile, block + 1, LANES - 1)
                    moved = rolled(offset, tile, block, LANES - 1)
                    plus_z = jnp.where(lane == LANES - 1, carry_in, moved)
                    minus = (load(offset - 1, tile, block), load(offset, tile, block, -1), minus_z)
                    plus = (load(offset + 1, tile, block), load(offset, tile, block, 1), plus_z)
                    rows = pl.ds(tile * SUBS, SUBS)
                    if coefs is None:
                        weight = [
                            held[index, plane - 1, block, rows, :]
                            for index in range(held.shape[0])
                        ]
                    else:
                        half = tile * SUBS % PACKED
                        key = ("coef", offset, tile * SUBS // PACKED, block)
                        if key not in kept:
                            packed = pl.ds(tile * SUBS - half, PACKED)
                            lanes = pl.ds(block * LANES, LANES)
                            kept[key] = [
                                coefs(field, plane, packed, lanes).astype(jnp.float32)
                                for field in range(FIELDS)
                            ]
                        mode = FIELDS if held is None else held.shape[0]
                        fields = [field[half : half + SUBS] for field in kept[key]]
                        weight = weights_of(mode, *fields)
                        if held is not None:
                            for index, value in enumerate(weight):
                                held[index, plane - 1, block, rows, :] = value
                    value = swept(load(offset, tile, block), minus, plus, weight)
                    if len(target.shape) == 4:
                        target[plane, block, pl.ds(FLOOR + tile * SUBS, SUBS), :] = value
                    else:
                        target[plane - shift, rows, pl.ds(block * LANES, LANES)] = value
        return carry

    assert (stop - first) % UNROLL == 0
    lax.fori_loop(0, (stop - first) // UNROLL, pair, 0)


def set_rims(grids, guess, per_plane, spots, height):
    for grid in grids:
        for block in range(grid.shape[1]):
            grid[:, block, pl.ds(0, FLOOR), :] = jnp.zeros(
                (grid.shape[0], FLOOR, LANES), jnp.float32
            )
    for at, plane in spots:
        for block in range(grids[0].shape[1]):
            line = ghost_line(guess, plane * per_plane, block)
            for grid in grids:
                grid[at, block, pl.ds(FLOOR + height, 1), :] = line


def set_edges(grids, parts, right_first, height):
    for side, first, fine_first in ((0, 0, REACH - FINE), (1, right_first, 0)):
        near = first + REACH - COEF_REACH if side == 0 else first
        for block in range(grids[0].shape[1]):
            lanes = pl.ds(block * LANES, LANES)
            for plane in range(REACH):
                value = parts[side][plane, :, lanes].astype(jnp.float32)
                if fine_first <= plane < fine_first + FINE:
                    rest = parts[side][REACH + plane - fine_first, :, lanes]
                    value = value + rest.astype(jnp.float32)
                grids[0][first + plane, block, pl.ds(FLOOR, height), :] = value
            tail = parts[side][SLOTS, pl.ds(0, PACKED), lanes].astype(jnp.float32)
            for plane in range(COEF_REACH):
                row = tail[plane : plane + 1]
                for part in (1, 2):
                    at = part * COEF_REACH + plane
                    row = row + tail[at : at + 1]
                for grid in grids:
                    grid[near + plane, block, pl.ds(FLOOR + height, 1), :] = row


def set_plane(grid, at, plain, plane, height):
    for block in range(grid.shape[1]):
        grid[at, block, pl.ds(FLOOR, height), :] = plain[plane, :, pl.ds(block * LANES, LANES)]


def strip_means(last, first, count):
    lane = lax.broadcasted_iota(jnp.int32, (count, LANES), 1)
    means = jnp.zeros((count, LANES), jnp.float32)
    strips = LANES // INTERFACE_STRIP
    for block in range(last.shape[2] // LANES):
        top = last[pl.ds(first, count), last.shape[1] - 1, pl.ds(block * LANES, LANES)]
        for strip in range(strips):
            mine = (lane >= strip * INTERFACE_STRIP) & (lane < (strip + 1) * INTERFACE_STRIP)
            total = jnp.sum(jnp.where(mine, top, 0.0), axis=1, keepdims=True)
            means = jnp.where(lane == block * strips + strip, total / INTERFACE_STRIP, means)
    return means


def set_face(means, face, across):
    line = lax.broadcasted_iota(jnp.int32, (LANES, LANES), 0)
    column = lax.broadcasted_iota(jnp.int32, (LANES, LANES), 1)
    spread_out = jnp.dot(
        means,
        jnp.where(column % across == line, 1.0, 0.0),
        precision=HIGHEST,
        preferred_element_type=jnp.float32,
    )
    per_row = LANES // across
    plane = lax.broadcasted_iota(jnp.int32, (per_row, LANES), 0)
    spot = lax.broadcasted_iota(jnp.int32, (per_row, LANES), 1) // across
    for row in range(face.shape[0]):
        mine = spread_out[row * per_row : (row + 1) * per_row]
        face[row] = jnp.sum(jnp.where(plane == spot, mine, 0.0), axis=0)


def inner_kernel(
    state, spread, flow, guess, out, edges, means, grid, other, plain, begin, rates, held, sems
):
    count, height = state.shape[0], state.shape[1]
    fetch = pltpu.make_async_copy(state, begin, sems.at[0])
    later = pltpu.make_async_copy(spread, rates, sems.at[1])
    fetch.start()
    later.start()

    def coefs(field, plane, rows, lanes):
        if field == 0:
            return rates[plane, rows, lanes]
        return flow[field - 1, plane, rows, lanes]

    spots = [(plane, plane) for plane in range(count)]
    set_rims((grid, other), guess, guess.shape[1] // count, spots, height)
    fetch.wait()
    for plane in range(count):
        set_plane(grid, plane, begin, plane, height)
    later.wait()
    pair = (grid, other)
    for step in range(1, SWEEPS):
        target = pair[step % 2]
        sweep(
            pair[(step + 1) % 2],
            target,
            coefs if step == 1 else None,
            held,
            height,
            step,
            count - step,
        )
        for index, plane in enumerate((step, step + 1, count - 2 - step, count - 1 - step)):
            edges[step - 1, index] = target[plane, :, pl.ds(FLOOR, height), :]
    source = pair[(SWEEPS + 1) % 2]
    sweep(source, plain, None, held, height, SWEEPS, count - SWEEPS, SWEEPS)
    push = pltpu.make_async_copy(plain, out.at[pl.ds(SWEEPS, count - 2 * SWEEPS)], sems.at[0])
    push.start()
    means[...] = strip_means(plain, 0, count - 2 * SWEEPS)
    push.wait()


def inner_field(state, spread, flow, guess):
    count, height, depth = state.shape
    lane_blocks = depth // LANES
    grid = pltpu.VMEM((count, lane_blocks, FLOOR + height + SUBS, LANES), jnp.float32)
    return pl.pallas_call(
        inner_kernel,
        out_shape=(
            jax.ShapeDtypeStruct(state.shape, jnp.float32),
            jax.ShapeDtypeStruct((SWEEPS - 1, 4, lane_blocks, height, LANES), jnp.float32),
            jax.ShapeDtypeStruct((count - 2 * SWEEPS, LANES), jnp.float32),
        ),
        in_specs=[ANY, ANY, WHOLE, SCALARS],
        out_specs=(pl.BlockSpec(memory_space=pltpu.HBM), WHOLE, WHOLE),
        scratch_shapes=[
            grid,
            grid,
            pltpu.VMEM((count - 2 * SWEEPS, height, depth), jnp.float32),
            pltpu.VMEM(state.shape, jnp.float32),
            pltpu.VMEM(spread.shape, spread.dtype),
            pltpu.VMEM((FIELDS, count - 2, lane_blocks, height, LANES), jnp.float32),
            pltpu.SemaphoreType.DMA((2,)),
        ],
        compiler_params=pltpu.CompilerParams(vmem_limit_bytes=24 * 2**20),
        cost_estimate=pl.CostEstimate(
            flops=50_000_000, bytes_accessed=20_000_000, transcendentals=0
        ),
        name="inner_field",
    )(state, spread, flow, guess)


def outer_kernel(
    state,
    spread,
    flow,
    guess,
    left,
    right,
    begun,
    edges,
    means,
    out,
    face,
    grid,
    other,
    plain,
    begin,
    rates,
    held,
    sems,
):
    count, height = state.shape[0], state.shape[1]
    lane_blocks = grid.shape[1]
    low, high = pl.ds(0, SWEEPS), pl.ds(SWEEPS, SWEEPS)
    last = pl.ds(count - SWEEPS, SWEEPS)
    fetch = [
        pltpu.make_async_copy(spread.at[low], rates.at[low], sems.at[0]),
        pltpu.make_async_copy(spread.at[last], rates.at[high], sems.at[1]),
        pltpu.make_async_copy(state.at[pl.ds(0, 2)], begin.at[pl.ds(0, 2)], sems.at[2]),
        pltpu.make_async_copy(state.at[pl.ds(count - 2, 2)], begin.at[pl.ds(2, 2)], sems.at[3]),
    ]
    start_all(fetch)

    def hold(at, planes):
        for block in range(lane_blocks):
            lanes = pl.ds(block * LANES, LANES)
            fields = [ref[(*spot, slice(None), lanes)].astype(jnp.float32) for ref, spot in planes]
            for index, value in enumerate(weights_of(FIELDS, *fields)):
                held[index, at, block] = value

    for message, first in ((left, 0), (right, count - 1)):
        for plane in range(COEF_REACH):
            slots = [REACH + FINE + field * COEF_REACH + plane for field in range(FIELDS)]
            hold(first + plane, [(message, (slot,)) for slot in slots])
    spots = [(REACH + plane, plane) for plane in range(SWEEPS)]
    spots += [(plane, plane) for plane in range(count - SWEEPS, count)]
    set_rims((grid, other), guess, guess.shape[1] // count, spots, height)
    set_edges((grid, other), (left, right), count, height)
    wait_all(fetch)
    for index, (at, plane) in enumerate(spots):
        hold(at - 1, [(rates, (index,))] + [(flow, (axis, plane)) for axis in range(3)])
    for plane in range(2):
        set_plane(grid, REACH + plane, begin, plane, height)
        set_plane(grid, count - 2 + plane, begin, 2 + plane, height)
    pair = (grid, other)
    for step in range(1, SWEEPS):
        source, target = pair[(step + 1) % 2], pair[step % 2]
        sweep(source, target, None, held, height, step, step + SWEEPS)
        right_first = count + REACH - SWEEPS - step
        sweep(source, target, None, held, height, right_first, right_first + SWEEPS)
        spots = (REACH + step, REACH + step + 1, count - 2 - step, count - 1 - step)
        for index, at in enumerate(spots):
            target[at, :, pl.ds(FLOOR, height), :] = edges[step - 1, index]
    source = pair[(SWEEPS + 1) % 2]
    pushes = []
    for index, first in enumerate((SWEEPS, count - SWEEPS)):
        kept = index * SWEEPS
        sweep(source, plain, None, held, height, first, first + SWEEPS, first - kept)
        final = 0 if index == 0 else count - SWEEPS
        pushes.append(
            pltpu.make_async_copy(
                plain.at[pl.ds(kept, SWEEPS)], out.at[pl.ds(final, SWEEPS)], sems.at[index]
            )
        )
        pushes[-1].start()
    whole = [strip_means(plain, 0, SWEEPS), means[...], strip_means(plain, SWEEPS, SWEEPS)]
    set_face(jnp.concatenate(whole, axis=0), face, state.shape[2] // INTERFACE_STRIP)
    wait_all(pushes)


def outer_field(state, spread, flow, guess, left, right, begun, edges, means):
    count, height, depth = state.shape
    lane_blocks = depth // LANES
    extended = count + REACH
    grid = pltpu.VMEM((extended, lane_blocks, FLOOR + height + SUBS, LANES), jnp.float32)
    return pl.pallas_call(
        outer_kernel,
        out_shape=(
            jax.ShapeDtypeStruct(state.shape, jnp.float32),
            jax.ShapeDtypeStruct((guess.shape[1] // LANES, LANES), jnp.float32),
        ),
        in_specs=[
            ANY,
            ANY,
            WHOLE,
            SCALARS,
            *[WHOLE] * 2,
            pl.BlockSpec(memory_space=pltpu.HBM),
            *[WHOLE] * 2,
        ],
        out_specs=(pl.BlockSpec(memory_space=pltpu.HBM), WHOLE),
        input_output_aliases={6: 0},
        scratch_shapes=[
            grid,
            grid,
            pltpu.VMEM((2 * SWEEPS, height, depth), jnp.float32),
            pltpu.VMEM((4, height, depth), jnp.float32),
            pltpu.VMEM((2 * SWEEPS, height, depth), spread.dtype),
            pltpu.VMEM((FIELDS, extended - 2, lane_blocks, height, LANES), jnp.float32),
            pltpu.SemaphoreType.DMA((4,)),
        ],
        compiler_params=pltpu.CompilerParams(vmem_limit_bytes=24 * 2**20),
        cost_estimate=pl.CostEstimate(
            flops=35_000_000, bytes_accessed=15_000_000, transcendentals=0
        ),
        name="outer_field",
    )(state, spread, flow, guess, left, right, begun, edges, means)


def gram_kernel(panel, gram):
    value = panel[...]
    gram[...] = lax.dot_general(
        value,
        value,
        (((0,), (0,)), ((), ())),
        precision=HIGHEST,
        preferred_element_type=jnp.float32,
    )


def local_gram(panel):
    columns = panel.shape[1]
    return pl.pallas_call(
        gram_kernel,
        out_shape=jax.ShapeDtypeStruct((columns, columns), jnp.float32),
        in_specs=[WHOLE],
        out_specs=WHOLE,
        compiler_params=SMALL,
        cost_estimate=pl.CostEstimate(flops=9_000_000, bytes_accessed=200_000, transcendentals=0),
        name="gram",
    )(panel)


def sum_kernel(parts, *rest):
    *extra, sent = rest
    total = jnp.sum(parts[...], axis=0)
    if extra:
        lines = extra[0][...]
        pad = jnp.zeros((SUBS - lines.shape[0], lines.shape[1]), jnp.float32)
        total = jnp.concatenate([total, lines, pad], axis=0)
    for copy in range(sent.shape[0]):
        sent[copy] = total


def sum_and_copy(name, receivers, parts, *extra):
    _, rows, columns = parts.shape
    rows += SUBS if extra else 0
    return pl.pallas_call(
        sum_kernel,
        out_shape=jax.ShapeDtypeStruct((receivers, rows, columns), jnp.float32),
        in_specs=[WHOLE] * (1 + len(extra)),
        out_specs=WHOLE,
        compiler_params=SMALL,
        cost_estimate=pl.CostEstimate(flops=100_000, bytes_accessed=500_000, transcendentals=0),
        name=name,
    )(parts, *extra)


def tilde_kernel(gathered, partner_rows, guess, panel, tilde, sent):
    lines = guess.shape[1] // LANES
    first = gathered.shape[1] - SUBS
    table = jnp.concatenate(
        [gathered[slab, pl.ds(first, lines), :] for slab in range(gathered.shape[0])], axis=0
    )
    wanted = partner_rows[...]
    line = lax.broadcasted_iota(jnp.int32, (table.shape[0], wanted.shape[1]), 0)
    chosen = jnp.where(line == wanted // LANES, 1.0, 0.0)
    picked = lax.dot_general(
        table,
        chosen,
        (((0,), (0,)), ((), ())),
        precision=HIGHEST,
        preferred_element_type=jnp.float32,
    )
    spot = lax.broadcasted_iota(jnp.int32, picked.shape, 0)
    values = jnp.sum(jnp.where(spot == wanted % LANES, picked, 0.0), axis=0, keepdims=True)
    tilde[...] = values
    projection = jnp.dot(
        values - guess[...],
        panel[...],
        precision=HIGHEST,
        preferred_element_type=jnp.float32,
    )
    sent[...] = jnp.broadcast_to(projection[None], sent.shape)


def tilde_and_projection(gathered, partner_rows, guess, panel, receivers):
    return pl.pallas_call(
        tilde_kernel,
        out_shape=(
            jax.ShapeDtypeStruct(guess.shape, jnp.float32),
            jax.ShapeDtypeStruct((receivers, 1, panel.shape[1]), jnp.float32),
        ),
        in_specs=[WHOLE] * 4,
        out_specs=(WHOLE,) * 2,
        compiler_params=SMALL,
        cost_estimate=pl.CostEstimate(flops=9_000_000, bytes_accessed=900_000, transcendentals=0),
        name="tilde",
    )(gathered, partner_rows, guess, panel)


def small_inverse(block):
    size = len(block)
    left = [list(row) for row in block]
    unit = [[None] * size for _ in range(size)]
    reciprocals = []
    for a in range(size):
        reciprocal = 1.0 / left[a][a]
        reciprocals.append(reciprocal)
        for row in range(a + 1, size):
            factor = left[row][a] * reciprocal
            for column in range(a + 1, row + 1):
                left[row][column] = left[row][column] - factor * left[column][a]
            for column in range(a):
                known = unit[row][column]
                change = factor * unit[a][column]
                unit[row][column] = -change if known is None else known - change
            unit[row][a] = -factor
    return unit, reciprocals


def column_of(entries):
    sub = lax.broadcasted_iota(jnp.int32, (SUBS, LANES), 0)
    column = jnp.zeros((SUBS, LANES), jnp.float32)
    for row, entry in enumerate(entries):
        if entry is not None:
            column = jnp.where(sub == row, entry, column)
    return column


def inverse_factor(tiles):
    shape = (SUBS, LANES)
    lane = lax.broadcasted_iota(jnp.int32, shape, 1)
    sub = lax.broadcasted_iota(jnp.int32, shape, 0)
    tiles = list(tiles)
    done = []
    for home in range(len(tiles)):
        first = home * SUBS
        columns = [
            [
                jnp.broadcast_to(tile[:, first + b : first + b + 1], shape)
                for b in range(SUBS)
            ]
            for tile in tiles[home:]
        ]
        block = [
            [jnp.broadcast_to(columns[0][b][a : a + 1], shape) for b in range(a + 1)]
            for a in range(SUBS)
        ]
        panel = (lane >= first) & (lane < first + SUBS)
        own = jnp.where(panel, jnp.where(lane - first == sub, 1.0, 0.0), tiles[home])
        lines = [jnp.broadcast_to(own[a : a + 1], shape) for a in range(SUBS)]
        unit, reciprocals = small_inverse(block)
        result = own
        for b in range(SUBS - 1):
            result = result + column_of([unit[a][b] for a in range(SUBS)]) * lines[b]
        roots = jnp.sqrt(column_of(reciprocals))
        done.append(jnp.where(lane <= sub + first, result, 0.0) * roots)
        if home + 1 == len(tiles):
            break
        answers = [
            jnp.broadcast_to(result[a : a + 1], shape) * reciprocals[a] for a in range(SUBS)
        ]
        for index in range(home + 1, len(tiles)):
            tile = jnp.where(panel, 0.0, tiles[index])
            raw = columns[index - home]
            parts = []
            for a in range(SUBS):
                factor = raw[a]
                for b in range(a):
                    factor = factor + unit[a][b] * raw[b]
                parts.append(factor * answers[a])
            while len(parts) > 1:
                parts = [one + two for one, two in zip(parts[::2], parts[1::2])]
            tiles[index] = tile - parts[0]
    return done


def factor_kernel(total_rows, gathered, panel, changes, inverse_out, basis, turned):
    slabs, rows, _ = gathered.shape
    tiles = [
        gathered[slab, pl.ds(first, SUBS), :]
        for slab in range(slabs)
        for first in range(0, rows - SUBS, SUBS)
    ]
    inverse = jnp.concatenate(inverse_factor(tiles), axis=0)
    inverse_out[...] = inverse
    turned[...] = lax.dot_general(
        changes[...],
        inverse,
        (((1,), (1,)), ((), ())),
        precision=HIGHEST,
        preferred_element_type=jnp.float32,
    )
    basis[...] = lax.dot_general(
        panel[...],
        inverse * math.sqrt(total_rows),
        (((1,), (1,)), ((), ())),
        precision=HIGHEST,
        preferred_element_type=jnp.float32,
    )


def factor_and_basis(total_rows, gathered, panel, changes):
    columns = panel.shape[1]
    return pl.pallas_call(
        functools.partial(factor_kernel, total_rows),
        out_shape=(
            jax.ShapeDtypeStruct((columns, columns), jnp.float32),
            jax.ShapeDtypeStruct(panel.shape, jnp.float32),
            jax.ShapeDtypeStruct(changes.shape, jnp.float32),
        ),
        in_specs=[WHOLE] * 3,
        out_specs=(WHOLE,) * 3,
        compiler_params=SMALL,
        cost_estimate=pl.CostEstimate(flops=30_000_000, bytes_accessed=9_000_000, transcendentals=0),
        name="factor",
    )(gathered, panel, changes)


def update_kernel(parts, inverse, turned, tilde, guess):
    projection = jnp.sum(parts[...], axis=0)
    across = (((1,), (1,)), ((), ()))
    half = lax.dot_general(
        projection, inverse[...], across, precision=HIGHEST, preferred_element_type=jnp.float32
    )
    guess[...] = tilde[...] - lax.dot_general(
        half, turned[...], across, precision=HIGHEST, preferred_element_type=jnp.float32
    )


def update(parts, inverse, turned, tilde):
    return pl.pallas_call(
        update_kernel,
        out_shape=jax.ShapeDtypeStruct(tilde.shape, jnp.float32),
        in_specs=[WHOLE] * 4,
        out_specs=WHOLE,
        compiler_params=SMALL,
        cost_estimate=pl.CostEstimate(flops=9_000_000, bytes_accessed=400_000, transcendentals=0),
        name="update",
    )(parts, inverse, turned, tilde)


def shards(
    thermal_state,
    thermal_spreading_rate,
    flow_speed_vector,
    interface_guess,
    partner_facing_rows,
    mismatch_change_matrix,
    output_change_matrix,
):
    state = thermal_state[0]
    spread = thermal_spreading_rate[0]
    flow = flow_speed_vector[:, 0]
    panel = mismatch_change_matrix[0]
    far = [
        pltpu.with_memory_space_constraint(value, pltpu.HBM) for value in (state, spread, flow)
    ]
    slabs = lax.axis_size("slab")
    wide = lax.axis_size("half") * lax.axis_size("pair")

    everyone = ("half", "pair", "slab")
    onward = [(i, i + 1) for i in range(slabs - 1)]
    back = [(i + 1, i) for i in range(slabs - 1)]

    gram = local_gram(panel).reshape(slabs, -1, panel.shape[1])
    gram, far[1] = lax.optimization_barrier((gram, far[1]))
    right, left = pack(*far, interface_guess)
    gram_parts = lax.all_to_all(gram, "slab", 0, 0, tiled=True)
    right, left, gram_parts = lax.optimization_barrier((right, left, gram_parts))
    from_left = lax.ppermute(right, "slab", onward)
    from_right = lax.ppermute(left, "slab", back)
    gram_parts = lax.all_to_all(
        sum_and_copy("sum_slab", wide, gram_parts), ("half", "pair"), 0, 0, tiled=True
    )
    begun, edges, means = inner_field(*far[:2], flow, interface_guess)
    temperature, face = outer_field(
        *far[:2], flow, interface_guess, from_left, from_right, begun, edges, means
    )
    face = lax.ppermute(face, "half", [(0, 1), (1, 0)])
    gathered = lax.all_to_all(
        sum_and_copy("sum_wide", slabs, gram_parts, face), "slab", 0, 0, tiled=True
    )
    tilde, share = tilde_and_projection(
        gathered, partner_facing_rows, interface_guess, panel, slabs * wide
    )
    share = lax.all_to_all(share, everyone, 0, 0, tiled=True)
    inverse, basis, turned = factor_and_basis(
        panel.shape[0] * slabs * wide, gathered, panel, output_change_matrix[0]
    )
    updated = update(share, inverse, turned, tilde)
    return temperature[None], updated, basis[None]


def solution(mesh):
    wide, slab = mesh.shape["wide"], mesh.shape["slab"]
    fine = Mesh(mesh.devices.reshape(2, wide // 2, slab), ("half", "pair", "slab"))
    parts = ("half", "pair")
    return jax.shard_map(
        shards,
        mesh=fine,
        in_specs=(
            P(parts, "slab", None, None),
            P(parts, "slab", None, None),
            P(None, parts, "slab", None, None),
            P(parts, "slab"),
            P(parts, "slab"),
            P(parts, "slab", None),
            P(parts, "slab", None),
        ),
        out_specs=(P(parts, "slab", None, None), P(parts, "slab"), P(parts, "slab", None)),
        check_vma=False,
    )
```

```python
import functools
import math

import jax
import jax.numpy as jnp
from jax import lax
from jax.experimental import pallas as pl
from jax.experimental.pallas import tpu as pltpu
from jax.sharding import Mesh
from jax.sharding import PartitionSpec as P

INTERFACE_STRIP = 64
SWEEPS = 4
STEP_SIZE = 0.11
PACKED = 16
LANES = 128
SUBS = 8
REACH = SWEEPS
COEF_REACH = SWEEPS - 1
FINE = 1
FIELDS = 4
SLOTS = REACH + FINE + FIELDS * COEF_REACH
HIGHEST = lax.Precision.HIGHEST
ANY = pl.BlockSpec(memory_space=pl.ANY)
WHOLE = pl.BlockSpec(memory_space=pltpu.VMEM)
SMALL = pltpu.CompilerParams(vmem_limit_bytes=8 * 2**20)
SCALARS = pl.BlockSpec(memory_space=pltpu.SMEM)


def start_all(copies):
    for copy in copies:
        copy.start()


def wait_all(copies):
    for copy in copies:
        copy.wait()


def ghost_line(guess, first, block, in_lanes=False):
    lane = lax.broadcasted_iota(jnp.int32, (1, LANES), 1)
    strips = LANES // INTERFACE_STRIP
    at = first + block * strips
    def value(strip):
        if in_lanes:
            spot = guess[:, pl.ds(at // LANES * LANES, LANES)]
            own = at % LANES + strip
            return jnp.broadcast_to(spot[:, own : own + 1], (1, LANES))
        return guess[0, at + strip]

    row = jnp.broadcast_to(value(0), (1, LANES))
    for strip in range(1, strips):
        row = jnp.where(lane < strip * INTERFACE_STRIP, row, value(strip))
    return row


def pack_kernel(
    state, spread, flow, guess, right_out, left_out, right, left, planes, sems
):
    count = state.shape[0]
    lane_blocks = state.shape[2] // LANES
    per_plane = guess.shape[1] // count
    fetch = [
        pltpu.make_async_copy(state.at[pl.ds(count - REACH, REACH)], planes.at[0], sems.at[8]),
        pltpu.make_async_copy(state.at[pl.ds(0, REACH)], planes.at[1], sems.at[9]),
    ]
    started = []
    for side, out, first in ((0, right, count - COEF_REACH), (1, left, 0)):
        source = [spread.at[pl.ds(first, COEF_REACH)]]
        source += [flow.at[axis, pl.ds(first, COEF_REACH)] for axis in range(3)]
        for field in range(FIELDS):
            slot = REACH + FINE + field * COEF_REACH
            started.append(
                pltpu.make_async_copy(
                    source[field],
                    out.at[pl.ds(slot, COEF_REACH)],
                    sems.at[side * FIELDS + field],
                )
            )
    start_all(fetch)
    start_all(started)
    for out, first in ((right, count - COEF_REACH), (left, 0)):
        for block in range(lane_blocks):
            lines = [
                ghost_line(guess, (first + plane) * per_plane, block, in_lanes=True)
                for plane in range(COEF_REACH)
            ]
            pieces = []
            for _ in range(3):
                leads = [line.astype(jnp.bfloat16).astype(jnp.float32) for line in lines]
                lines = [line - lead for line, lead in zip(lines, leads)]
                pieces += leads
            pad = jnp.zeros((PACKED - 3 * COEF_REACH, LANES), jnp.float32)
            whole = jnp.concatenate([*pieces, pad], axis=0).astype(jnp.bfloat16)
            out[SLOTS, pl.ds(0, PACKED), pl.ds(block * LANES, LANES)] = whole
        unused = state.shape[1] - PACKED
        out[SLOTS, pl.ds(PACKED, unused), :] = jnp.zeros((unused, state.shape[2]), jnp.bfloat16)
    wait_all(fetch)
    for side, out, fine_first in ((0, right, REACH - FINE), (1, left, 0)):
        for plane in range(REACH):
            value = planes[side, plane]
            lead = value.astype(jnp.bfloat16)
            out[plane] = lead
            if fine_first <= plane < fine_first + FINE:
                rest = value - lead.astype(jnp.float32)
                out[REACH + plane - fine_first] = rest.astype(jnp.bfloat16)
    wait_all(started)
    pushes = [
        pltpu.make_async_copy(right, right_out, sems.at[8]),
        pltpu.make_async_copy(left, left_out, sems.at[9]),
    ]
    start_all(pushes)
    wait_all(pushes)


def pack(state, spread, flow, guess):
    message = jax.ShapeDtypeStruct((SLOTS + 1, *state.shape[1:]), jnp.bfloat16)
    return pl.pallas_call(
        pack_kernel,
        out_shape=(pltpu.HBM(message.shape, message.dtype),) * 2,
        in_specs=[ANY, ANY, ANY, WHOLE],
        out_specs=(pl.BlockSpec(memory_space=pltpu.HBM),) * 2,
        scratch_shapes=[
            pltpu.VMEM(message.shape, message.dtype),
            pltpu.VMEM(message.shape, message.dtype),
            pltpu.VMEM((2, REACH, *state.shape[1:]), jnp.float32),
            pltpu.SemaphoreType.DMA((10,)),
        ],
        compiler_params=pltpu.CompilerParams(vmem_limit_bytes=16 * 2**20),
        cost_estimate=pl.CostEstimate(flops=2_000_000, bytes_accessed=9_000_000, transcendentals=0),
        name="pack_edges",
    )(state, spread, flow, guess)


def weights_of(mode, rate, flow_x, flow_y, flow_z):
    rate = STEP_SIZE * rate
    flow_x, flow_y, flow_z = (0.5 * STEP_SIZE * flow for flow in (flow_x, flow_y, flow_z))
    if mode == 4:
        return rate, flow_x, flow_y, flow_z
    return (
        rate + flow_x,
        rate - flow_x,
        rate + flow_y,
        rate - flow_y,
        rate + flow_z,
        rate - flow_z,
        1.0 - 6.0 * rate,
    )


def swept(here, minus, plus, weight):
    if len(weight) == 4:
        total = ((plus[0] + minus[0]) + (plus[1] + minus[1])) + (plus[2] + minus[2])
        carried = (
            weight[1] * (plus[0] - minus[0])
            + weight[2] * (plus[1] - minus[1])
            + weight[3] * (plus[2] - minus[2])
        )
        return here + (weight[0] * (total - 6.0 * here) - carried)
    x, y, z = (
        weight[2 * axis] * minus[axis] + weight[2 * axis + 1] * plus[axis] for axis in range(3)
    )
    return (x + y) + (z + weight[6] * here)


FLOOR = 8


def sweep(source, target, coefs, held, height, first, stop, shift=0, unroll=2):
    lane_blocks = source.shape[1]
    lane = lax.broadcasted_iota(jnp.int32, (SUBS, LANES), 1)
    zero = jnp.zeros((SUBS, LANES), jnp.float32)

    def pair(step, carry):
        low = first + step * unroll
        kept = {}

        def load(offset, tile, block, shift=0):
            key = (offset, tile, block, shift)
            if key not in kept:
                rows = pl.ds(FLOOR + tile * SUBS + shift, SUBS)
                kept[key] = source[low + offset, block, rows, :]
            return kept[key]

        def rolled(offset, tile, block, shift):
            key = ("rolled", offset, tile, block, shift)
            if key not in kept:
                kept[key] = pltpu.roll(load(offset, tile, block), shift, 1)
            return kept[key]

        for block in range(lane_blocks):
            for tile in range(height // SUBS):
                for offset in range(unroll):
                    plane = low + offset
                    carry_in = rolled(offset, tile, block - 1, 1) if block else zero
                    minus_z = jnp.where(lane == 0, carry_in, rolled(offset, tile, block, 1))
                    last = block + 1 == lane_blocks
                    carry_in = zero if last else rolled(offset, tile, block + 1, LANES - 1)
                    moved = rolled(offset, tile, block, LANES - 1)
                    plus_z = jnp.where(lane == LANES - 1, carry_in, moved)
                    minus = (load(offset - 1, tile, block), load(offset, tile, block, -1), minus_z)
                    plus = (load(offset + 1, tile, block), load(offset, tile, block, 1), plus_z)
                    rows = pl.ds(tile * SUBS, SUBS)
                    if coefs is None:
                        weight = [
                            held[index, plane - 1, block, rows, :]
                            for index in range(held.shape[0])
                        ]
                    else:
                        half = tile * SUBS % PACKED
                        key = ("coef", offset, tile * SUBS // PACKED, block)
                        if key not in kept:
                            packed = pl.ds(tile * SUBS - half, PACKED)
                            lanes = pl.ds(block * LANES, LANES)
                            kept[key] = [
                                coefs(field, plane, packed, lanes).astype(jnp.float32)
                                for field in range(FIELDS)
                            ]
                        mode = FIELDS if held is None else held.shape[0]
                        fields = [field[half : half + SUBS] for field in kept[key]]
                        weight = weights_of(mode, *fields)
                        if held is not None:
                            for index, value in enumerate(weight):
                                held[index, plane - 1, block, rows, :] = value
                    value = swept(load(offset, tile, block), minus, plus, weight)
                    if len(target.shape) == 4:
                        target[plane, block, pl.ds(FLOOR + tile * SUBS, SUBS), :] = value
                    else:
                        target[plane - shift, rows, pl.ds(block * LANES, LANES)] = value
        return carry

    assert (stop - first) % unroll == 0
    lax.fori_loop(0, (stop - first) // unroll, pair, 0)


def set_rims(grids, guess, per_plane, spots, height):
    for grid in grids:
        for block in range(grid.shape[1]):
            grid[:, block, pl.ds(0, FLOOR), :] = jnp.zeros(
                (grid.shape[0], FLOOR, LANES), jnp.float32
            )
    for at, plane in spots:
        for block in range(grids[0].shape[1]):
            line = ghost_line(guess, plane * per_plane, block)
            for grid in grids:
                grid[at, block, pl.ds(FLOOR + height, 1), :] = line


def set_edges(grids, parts, right_first, height):
    for side, first, fine_first in ((0, 0, REACH - FINE), (1, right_first, 0)):
        near = first + REACH - COEF_REACH if side == 0 else first
        for block in range(grids[0].shape[1]):
            lanes = pl.ds(block * LANES, LANES)
            for plane in range(REACH):
                value = parts[side][plane, :, lanes].astype(jnp.float32)
                if fine_first <= plane < fine_first + FINE:
                    rest = parts[side][REACH + plane - fine_first, :, lanes]
                    value = value + rest.astype(jnp.float32)
                grids[0][first + plane, block, pl.ds(FLOOR, height), :] = value
            tail = parts[side][SLOTS, pl.ds(0, PACKED), lanes].astype(jnp.float32)
            for plane in range(COEF_REACH):
                row = tail[plane : plane + 1]
                for part in (1, 2):
                    at = part * COEF_REACH + plane
                    row = row + tail[at : at + 1]
                for grid in grids:
                    grid[near + plane, block, pl.ds(FLOOR + height, 1), :] = row


def set_plane(grid, at, plain, plane, height):
    for block in range(grid.shape[1]):
        grid[at, block, pl.ds(FLOOR, height), :] = plain[plane, :, pl.ds(block * LANES, LANES)]


def strip_means(last, first, count):
    lane = lax.broadcasted_iota(jnp.int32, (count, LANES), 1)
    means = jnp.zeros((count, LANES), jnp.float32)
    strips = LANES // INTERFACE_STRIP
    for block in range(last.shape[2] // LANES):
        top = last[pl.ds(first, count), last.shape[1] - 1, pl.ds(block * LANES, LANES)]
        for strip in range(strips):
            mine = (lane >= strip * INTERFACE_STRIP) & (lane < (strip + 1) * INTERFACE_STRIP)
            total = jnp.sum(jnp.where(mine, top, 0.0), axis=1, keepdims=True)
            means = jnp.where(lane == block * strips + strip, total / INTERFACE_STRIP, means)
    return means


def set_face(means, face, across):
    line = lax.broadcasted_iota(jnp.int32, (LANES, LANES), 0)
    column = lax.broadcasted_iota(jnp.int32, (LANES, LANES), 1)
    spread_out = jnp.dot(
        means,
        jnp.where(column % across == line, 1.0, 0.0),
        precision=HIGHEST,
        preferred_element_type=jnp.float32,
    )
    per_row = LANES // across
    plane = lax.broadcasted_iota(jnp.int32, (per_row, LANES), 0)
    spot = lax.broadcasted_iota(jnp.int32, (per_row, LANES), 1) // across
    for row in range(face.shape[0]):
        mine = spread_out[row * per_row : (row + 1) * per_row]
        face[row] = jnp.sum(jnp.where(plane == spot, mine, 0.0), axis=0)


def inner_kernel(
    state, spread, flow, guess, out, edges, means, grid, other, plain, begin, rates, held, sems
):
    count, height = state.shape[0], state.shape[1]
    fetch = pltpu.make_async_copy(state, begin, sems.at[0])
    later = pltpu.make_async_copy(spread, rates, sems.at[1])
    fetch.start()
    later.start()

    def coefs(field, plane, rows, lanes):
        if field == 0:
            return rates[plane, rows, lanes]
        return flow[field - 1, plane, rows, lanes]

    spots = [(plane, plane) for plane in range(count)]
    set_rims((grid, other), guess, guess.shape[1] // count, spots, height)
    fetch.wait()
    for plane in range(count):
        set_plane(grid, plane, begin, plane, height)
    later.wait()
    pair = (grid, other)
    for step in range(1, SWEEPS):
        target = pair[step % 2]
        sweep(
            pair[(step + 1) % 2],
            target,
            coefs if step == 1 else None,
            held,
            height,
            step,
            count - step,
        )
        for index, plane in enumerate((step, step + 1, count - 2 - step, count - 1 - step)):
            edges[step - 1, index] = target[plane, :, pl.ds(FLOOR, height), :]
    source = pair[(SWEEPS + 1) % 2]
    sweep(source, plain, None, held, height, SWEEPS, count - SWEEPS, SWEEPS)
    push = pltpu.make_async_copy(plain, out.at[pl.ds(SWEEPS, count - 2 * SWEEPS)], sems.at[0])
    push.start()
    means[...] = strip_means(plain, 0, count - 2 * SWEEPS)
    push.wait()


def inner_field(state, spread, flow, guess):
    count, height, depth = state.shape
    lane_blocks = depth // LANES
    grid = pltpu.VMEM((count, lane_blocks, FLOOR + height + SUBS, LANES), jnp.float32)
    return pl.pallas_call(
        inner_kernel,
        out_shape=(
            jax.ShapeDtypeStruct(state.shape, jnp.float32),
            jax.ShapeDtypeStruct((SWEEPS - 1, 4, lane_blocks, height, LANES), jnp.float32),
            jax.ShapeDtypeStruct((count - 2 * SWEEPS, LANES), jnp.float32),
        ),
        in_specs=[ANY, ANY, WHOLE, SCALARS],
        out_specs=(pl.BlockSpec(memory_space=pltpu.HBM), WHOLE, WHOLE),
        scratch_shapes=[
            grid,
            grid,
            pltpu.VMEM((count - 2 * SWEEPS, height, depth), jnp.float32),
            pltpu.VMEM(state.shape, jnp.float32),
            pltpu.VMEM(spread.shape, spread.dtype),
            pltpu.VMEM((FIELDS, count - 2, lane_blocks, height, LANES), jnp.float32),
            pltpu.SemaphoreType.DMA((2,)),
        ],
        compiler_params=pltpu.CompilerParams(vmem_limit_bytes=24 * 2**20),
        cost_estimate=pl.CostEstimate(
            flops=50_000_000, bytes_accessed=20_000_000, transcendentals=0
        ),
        name="inner_field",
    )(state, spread, flow, guess)


def outer_kernel(
    state,
    spread,
    flow,
    guess,
    left,
    right,
    begun,
    edges,
    means,
    out,
    face,
    grid,
    other,
    plain,
    begin,
    rates,
    held,
    sems,
):
    count, height = state.shape[0], state.shape[1]
    lane_blocks = grid.shape[1]
    low, high = pl.ds(0, SWEEPS), pl.ds(SWEEPS, SWEEPS)
    last = pl.ds(count - SWEEPS, SWEEPS)
    fetch = [
        pltpu.make_async_copy(spread.at[low], rates.at[low], sems.at[0]),
        pltpu.make_async_copy(spread.at[last], rates.at[high], sems.at[1]),
        pltpu.make_async_copy(state.at[pl.ds(0, 2)], begin.at[pl.ds(0, 2)], sems.at[2]),
        pltpu.make_async_copy(state.at[pl.ds(count - 2, 2)], begin.at[pl.ds(2, 2)], sems.at[3]),
    ]
    start_all(fetch)

    def hold(at, planes):
        for block in range(lane_blocks):
            lanes = pl.ds(block * LANES, LANES)
            fields = [ref[(*spot, slice(None), lanes)].astype(jnp.float32) for ref, spot in planes]
            for index, value in enumerate(weights_of(FIELDS, *fields)):
                held[index, at, block] = value

    for message, first in ((left, 0), (right, count - 1)):
        for plane in range(COEF_REACH):
            slots = [REACH + FINE + field * COEF_REACH + plane for field in range(FIELDS)]
            hold(first + plane, [(message, (slot,)) for slot in slots])
    spots = [(REACH + plane, plane) for plane in range(SWEEPS)]
    spots += [(plane, plane) for plane in range(count - SWEEPS, count)]
    set_rims((grid, other), guess, guess.shape[1] // count, spots, height)
    set_edges((grid, other), (left, right), count, height)
    wait_all(fetch)
    for index, (at, plane) in enumerate(spots):
        hold(at - 1, [(rates, (index,))] + [(flow, (axis, plane)) for axis in range(3)])
    for plane in range(2):
        set_plane(grid, REACH + plane, begin, plane, height)
        set_plane(grid, count - 2 + plane, begin, 2 + plane, height)
    pair = (grid, other)
    for step in range(1, SWEEPS):
        source, target = pair[(step + 1) % 2], pair[step % 2]
        sweep(source, target, None, held, height, step, step + SWEEPS, unroll=SWEEPS)
        right_first = count + REACH - SWEEPS - step
        sweep(
            source, target, None, held, height, right_first, right_first + SWEEPS, unroll=SWEEPS
        )
        spots = (REACH + step, REACH + step + 1, count - 2 - step, count - 1 - step)
        for index, at in enumerate(spots):
            target[at, :, pl.ds(FLOOR, height), :] = edges[step - 1, index]
    source = pair[(SWEEPS + 1) % 2]
    pushes = []
    for index, first in enumerate((SWEEPS, count - SWEEPS)):
        kept = index * SWEEPS
        sweep(source, plain, None, held, height, first, first + SWEEPS, first - kept, SWEEPS)
        final = 0 if index == 0 else count - SWEEPS
        pushes.append(
            pltpu.make_async_copy(
                plain.at[pl.ds(kept, SWEEPS)], out.at[pl.ds(final, SWEEPS)], sems.at[index]
            )
        )
        pushes[-1].start()
    whole = [strip_means(plain, 0, SWEEPS), means[...], strip_means(plain, SWEEPS, SWEEPS)]
    set_face(jnp.concatenate(whole, axis=0), face, state.shape[2] // INTERFACE_STRIP)
    wait_all(pushes)


def outer_field(state, spread, flow, guess, left, right, begun, edges, means):
    count, height, depth = state.shape
    lane_blocks = depth // LANES
    extended = count + REACH
    grid = pltpu.VMEM((extended, lane_blocks, FLOOR + height + SUBS, LANES), jnp.float32)
    return pl.pallas_call(
        outer_kernel,
        out_shape=(
            jax.ShapeDtypeStruct(state.shape, jnp.float32),
            jax.ShapeDtypeStruct((guess.shape[1] // LANES, LANES), jnp.float32),
        ),
        in_specs=[
            ANY,
            ANY,
            WHOLE,
            SCALARS,
            *[WHOLE] * 2,
            pl.BlockSpec(memory_space=pltpu.HBM),
            *[WHOLE] * 2,
        ],
        out_specs=(pl.BlockSpec(memory_space=pltpu.HBM), WHOLE),
        input_output_aliases={6: 0},
        scratch_shapes=[
            grid,
            grid,
            pltpu.VMEM((2 * SWEEPS, height, depth), jnp.float32),
            pltpu.VMEM((4, height, depth), jnp.float32),
            pltpu.VMEM((2 * SWEEPS, height, depth), spread.dtype),
            pltpu.VMEM((FIELDS, extended - 2, lane_blocks, height, LANES), jnp.float32),
            pltpu.SemaphoreType.DMA((4,)),
        ],
        compiler_params=pltpu.CompilerParams(vmem_limit_bytes=24 * 2**20),
        cost_estimate=pl.CostEstimate(
            flops=35_000_000, bytes_accessed=15_000_000, transcendentals=0
        ),
        name="outer_field",
    )(state, spread, flow, guess, left, right, begun, edges, means)


def gram_kernel(panel, gram):
    value = panel[...]
    gram[...] = lax.dot_general(
        value,
        value,
        (((0,), (0,)), ((), ())),
        precision=HIGHEST,
        preferred_element_type=jnp.float32,
    )


def local_gram(panel):
    columns = panel.shape[1]
    return pl.pallas_call(
        gram_kernel,
        out_shape=jax.ShapeDtypeStruct((columns, columns), jnp.float32),
        in_specs=[WHOLE],
        out_specs=WHOLE,
        compiler_params=SMALL,
        cost_estimate=pl.CostEstimate(flops=9_000_000, bytes_accessed=200_000, transcendentals=0),
        name="gram",
    )(panel)


def sum_kernel(parts, *rest):
    *extra, sent = rest
    total = jnp.sum(parts[...], axis=0)
    if extra:
        lines = extra[0][...]
        pad = jnp.zeros((SUBS - lines.shape[0], lines.shape[1]), jnp.float32)
        total = jnp.concatenate([total, lines, pad], axis=0)
    for copy in range(sent.shape[0]):
        sent[copy] = total


def sum_and_copy(name, receivers, parts, *extra):
    _, rows, columns = parts.shape
    rows += SUBS if extra else 0
    return pl.pallas_call(
        sum_kernel,
        out_shape=jax.ShapeDtypeStruct((receivers, rows, columns), jnp.float32),
        in_specs=[WHOLE] * (1 + len(extra)),
        out_specs=WHOLE,
        compiler_params=SMALL,
        cost_estimate=pl.CostEstimate(flops=100_000, bytes_accessed=500_000, transcendentals=0),
        name=name,
    )(parts, *extra)


def tilde_kernel(gathered, partner_rows, guess, panel, tilde, sent):
    lines = guess.shape[1] // LANES
    first = gathered.shape[1] - SUBS
    table = jnp.concatenate(
        [gathered[slab, pl.ds(first, lines), :] for slab in range(gathered.shape[0])], axis=0
    )
    wanted = partner_rows[...]
    line = lax.broadcasted_iota(jnp.int32, (table.shape[0], wanted.shape[1]), 0)
    chosen = jnp.where(line == wanted // LANES, 1.0, 0.0)
    picked = lax.dot_general(
        table,
        chosen,
        (((0,), (0,)), ((), ())),
        precision=HIGHEST,
        preferred_element_type=jnp.float32,
    )
    spot = lax.broadcasted_iota(jnp.int32, picked.shape, 0)
    values = jnp.sum(jnp.where(spot == wanted % LANES, picked, 0.0), axis=0, keepdims=True)
    tilde[...] = values
    projection = jnp.dot(
        values - guess[...],
        panel[...],
        precision=HIGHEST,
        preferred_element_type=jnp.float32,
    )
    sent[...] = jnp.broadcast_to(projection[None], sent.shape)


def tilde_and_projection(gathered, partner_rows, guess, panel, receivers):
    return pl.pallas_call(
        tilde_kernel,
        out_shape=(
            jax.ShapeDtypeStruct(guess.shape, jnp.float32),
            jax.ShapeDtypeStruct((receivers, 1, panel.shape[1]), jnp.float32),
        ),
        in_specs=[WHOLE] * 4,
        out_specs=(WHOLE,) * 2,
        compiler_params=SMALL,
        cost_estimate=pl.CostEstimate(flops=9_000_000, bytes_accessed=900_000, transcendentals=0),
        name="tilde",
    )(gathered, partner_rows, guess, panel)


def small_inverse(block):
    size = len(block)
    left = [list(row) for row in block]
    unit = [[None] * size for _ in range(size)]
    reciprocals = []
    for a in range(size):
        reciprocal = 1.0 / left[a][a]
        reciprocals.append(reciprocal)
        for row in range(a + 1, size):
            factor = left[row][a] * reciprocal
            for column in range(a + 1, row + 1):
                left[row][column] = left[row][column] - factor * left[column][a]
            for column in range(a):
                known = unit[row][column]
                change = factor * unit[a][column]
                unit[row][column] = -change if known is None else known - change
            unit[row][a] = -factor
    return unit, reciprocals


def column_of(entries):
    sub = lax.broadcasted_iota(jnp.int32, (SUBS, LANES), 0)
    column = jnp.zeros((SUBS, LANES), jnp.float32)
    for row, entry in enumerate(entries):
        if entry is not None:
            column = jnp.where(sub == row, entry, column)
    return column


def inverse_factor(tiles):
    shape = (SUBS, LANES)
    lane = lax.broadcasted_iota(jnp.int32, shape, 1)
    sub = lax.broadcasted_iota(jnp.int32, shape, 0)
    tiles = list(tiles)
    done = []
    for home in range(len(tiles)):
        first = home * SUBS
        columns = [
            [
                jnp.broadcast_to(tile[:, first + b : first + b + 1], shape)
                for b in range(SUBS)
            ]
            for tile in tiles[home:]
        ]
        block = [
            [jnp.broadcast_to(columns[0][b][a : a + 1], shape) for b in range(a + 1)]
            for a in range(SUBS)
        ]
        panel = (lane >= first) & (lane < first + SUBS)
        own = jnp.where(panel, jnp.where(lane - first == sub, 1.0, 0.0), tiles[home])
        lines = [jnp.broadcast_to(own[a : a + 1], shape) for a in range(SUBS)]
        unit, reciprocals = small_inverse(block)
        result = own
        for b in range(SUBS - 1):
            result = result + column_of([unit[a][b] for a in range(SUBS)]) * lines[b]
        roots = jnp.sqrt(column_of(reciprocals))
        done.append(jnp.where(lane <= sub + first, result, 0.0) * roots)
        if home + 1 == len(tiles):
            break
        answers = [
            jnp.broadcast_to(result[a : a + 1], shape) * reciprocals[a] for a in range(SUBS)
        ]
        for index in range(home + 1, len(tiles)):
            tile = jnp.where(panel, 0.0, tiles[index])
            raw = columns[index - home]
            parts = []
            for a in range(SUBS):
                factor = raw[a]
                for b in range(a):
                    factor = factor + unit[a][b] * raw[b]
                parts.append(factor * answers[a])
            while len(parts) > 1:
                parts = [one + two for one, two in zip(parts[::2], parts[1::2])]
            tiles[index] = tile - parts[0]
    return done


def factor_kernel(total_rows, gathered, panel, changes, inverse_out, basis, turned):
    slabs, rows, _ = gathered.shape
    tiles = [
        gathered[slab, pl.ds(first, SUBS), :]
        for slab in range(slabs)
        for first in range(0, rows - SUBS, SUBS)
    ]
    inverse = jnp.concatenate(inverse_factor(tiles), axis=0)
    inverse_out[...] = inverse
    turned[...] = lax.dot_general(
        changes[...],
        inverse,
        (((1,), (1,)), ((), ())),
        precision=HIGHEST,
        preferred_element_type=jnp.float32,
    )
    basis[...] = lax.dot_general(
        panel[...],
        inverse * math.sqrt(total_rows),
        (((1,), (1,)), ((), ())),
        precision=HIGHEST,
        preferred_element_type=jnp.float32,
    )


def factor_and_basis(total_rows, gathered, panel, changes):
    columns = panel.shape[1]
    return pl.pallas_call(
        functools.partial(factor_kernel, total_rows),
        out_shape=(
            jax.ShapeDtypeStruct((columns, columns), jnp.float32),
            jax.ShapeDtypeStruct(panel.shape, jnp.float32),
            jax.ShapeDtypeStruct(changes.shape, jnp.float32),
        ),
        in_specs=[WHOLE] * 3,
        out_specs=(WHOLE,) * 3,
        compiler_params=SMALL,
        cost_estimate=pl.CostEstimate(flops=30_000_000, bytes_accessed=9_000_000, transcendentals=0),
        name="factor",
    )(gathered, panel, changes)


def update_kernel(parts, inverse, turned, tilde, guess):
    projection = jnp.sum(parts[...], axis=0)
    across = (((1,), (1,)), ((), ()))
    half = lax.dot_general(
        projection, inverse[...], across, precision=HIGHEST, preferred_element_type=jnp.float32
    )
    guess[...] = tilde[...] - lax.dot_general(
        half, turned[...], across, precision=HIGHEST, preferred_element_type=jnp.float32
    )


def update(parts, inverse, turned, tilde):
    return pl.pallas_call(
        update_kernel,
        out_shape=jax.ShapeDtypeStruct(tilde.shape, jnp.float32),
        in_specs=[WHOLE] * 4,
        out_specs=WHOLE,
        compiler_params=SMALL,
        cost_estimate=pl.CostEstimate(flops=9_000_000, bytes_accessed=400_000, transcendentals=0),
        name="update",
    )(parts, inverse, turned, tilde)


def shards(
    thermal_state,
    thermal_spreading_rate,
    flow_speed_vector,
    interface_guess,
    partner_facing_rows,
    mismatch_change_matrix,
    output_change_matrix,
):
    state = thermal_state[0]
    spread = thermal_spreading_rate[0]
    flow = flow_speed_vector[:, 0]
    panel = mismatch_change_matrix[0]
    far = [
        pltpu.with_memory_space_constraint(value, pltpu.HBM) for value in (state, spread, flow)
    ]
    slabs = lax.axis_size("slab")
    wide = lax.axis_size("half") * lax.axis_size("pair")

    everyone = ("half", "pair", "slab")
    onward = [(i, i + 1) for i in range(slabs - 1)]
    back = [(i + 1, i) for i in range(slabs - 1)]

    gram = local_gram(panel).reshape(slabs, -1, panel.shape[1])
    gram, far[1] = lax.optimization_barrier((gram, far[1]))
    right, left = pack(*far, interface_guess)
    gram_parts = lax.all_to_all(gram, "slab", 0, 0, tiled=True)
    right, left, gram_parts = lax.optimization_barrier((right, left, gram_parts))
    from_left = lax.ppermute(right, "slab", onward)
    from_right = lax.ppermute(left, "slab", back)
    gram_parts = lax.all_to_all(
        sum_and_copy("sum_slab", wide, gram_parts), ("half", "pair"), 0, 0, tiled=True
    )
    begun, edges, means = inner_field(*far[:2], flow, interface_guess)
    temperature, face = outer_field(
        *far[:2], flow, interface_guess, from_left, from_right, begun, edges, means
    )
    face = lax.ppermute(face, "half", [(0, 1), (1, 0)])
    gathered = lax.all_to_all(
        sum_and_copy("sum_wide", slabs, gram_parts, face), "slab", 0, 0, tiled=True
    )
    tilde, share = tilde_and_projection(
        gathered, partner_facing_rows, interface_guess, panel, slabs * wide
    )
    share = lax.all_to_all(share, everyone, 0, 0, tiled=True)
    inverse, basis, turned = factor_and_basis(
        panel.shape[0] * slabs * wide, gathered, panel, output_change_matrix[0]
    )
    updated = update(share, inverse, turned, tilde)
    return temperature[None], updated, basis[None]


def solution(mesh):
    wide, slab = mesh.shape["wide"], mesh.shape["slab"]
    fine = Mesh(mesh.devices.reshape(2, wide // 2, slab), ("half", "pair", "slab"))
    parts = ("half", "pair")
    return jax.shard_map(
        shards,
        mesh=fine,
        in_specs=(
            P(parts, "slab", None, None),
            P(parts, "slab", None, None),
            P(None, parts, "slab", None, None),
            P(parts, "slab"),
            P(parts, "slab"),
            P(parts, "slab", None),
            P(parts, "slab", None),
        ),
        out_specs=(P(parts, "slab", None, None), P(parts, "slab"), P(parts, "slab", None)),
        check_vma=False,
    )
```
